32 devices in a mesh: sgroup: 8 (over z, y), tile: 4 (over x, core).
Axes of the slice: x: 2, y: 2, z: 4, core: 2. Of those that a mesh axis runs over, the one named last changes fastest.
Arguments:
- voltages: bfloat16 [2, 128, 256, 2, 16, 128], P(None, 'sgroup', 'tile'), may hold values from -6 to 6
- weights: bfloat16 [2, 128, 256, 2, 16], P(None, 'sgroup'), may hold values from -0.25 to 0.25
- antenna_slot_index: int32 [128, 256], P('sgroup', 'tile'), may hold values from 0 to 255, each once within a row
- station_order: int32 [128], replicated, may hold values from 0 to 127, each once
Outputs:
- visibilities: float32 [16, 2, 256, 256], P('tile', None, 'sgroup')
The draws below stay inside these ranges and needn't reach their ends.
Inputs may be any that keep to these rules, and one draw needn't show every extreme that they name: `station_order`: each station slot holds a different station. `antenna_slot_index`: within each station slot, each antenna slot holds a different antenna.
All inputs are finite; a program needn't handle non-finite values.
Results may differ from the reference program's by a relative error of at most 0.0038.
Values may be sent and summed in bfloat16 or wider, within the bound.
No kernel may reach another device: no remote copies, remote signals or barrier semaphores. Data moves between devices by JAX's collectives and lax.ppermute only.
A program may use at most 64 MiB of HBM per device.

```python
import jax
import jax.numpy as jnp
from jax import lax

ANTENNA_COUNT = 256
POLAR_COUNT = 2
CHANNEL_COUNT = 16
SPECTRA_COUNT = 128
STATION_COUNT = 128


def level_of(rng, extent, pieces, low, high):
    factor_of, own = 1.0, jax.random.fold_in(rng, 6)
    for position, blocks in pieces:
        heights = jnp.exp(jax.random.uniform(jax.random.fold_in(own, position), (blocks,), jnp.float32, low / len(pieces), high / len(pieces)))
        factor_of = factor_of * jnp.repeat(heights, extent[position] // blocks).reshape([-1 if axis == position else 1 for axis in range(len(extent))])
    return factor_of


def bell_draw(stream_key, dims, width, bound, cuts=(), held_as=jnp.bfloat16):
    entries = jax.random.normal(stream_key, dims, jnp.float32) * width
    if len(cuts) > 0:
        entries = level_of(stream_key, dims, cuts, -0.22, 0.18) * entries
    return jnp.clip(entries, min=-bound, max=bound).astype(held_as)


def setup_inputs(seed: int = 0) -> dict:
    key_list = jax.random.split(jax.random.key(seed), 5)
    return {
        "voltages": bell_draw(key_list[0], (2, STATION_COUNT, ANTENNA_COUNT, POLAR_COUNT, CHANNEL_COUNT, SPECTRA_COUNT), 1.0, 6.0, ((1, 8), (2, 4))),
        "weights": bell_draw(key_list[1], (2, STATION_COUNT, ANTENNA_COUNT, POLAR_COUNT, CHANNEL_COUNT), (2 * ANTENNA_COUNT) ** -0.5, 0.25, ((1, 8),)),
        "antenna_slot_index": jax.vmap(lambda own: jax.random.permutation(own, ANTENNA_COUNT))(jax.random.split(key_list[2], STATION_COUNT)).reshape((STATION_COUNT, ANTENNA_COUNT)).astype(jnp.int32),
        "station_order": jax.random.permutation(key_list[3], STATION_COUNT).astype(jnp.int32),
    }


def reference(voltages, weights, antenna_slot_index, station_order):
    stations = voltages.shape[1]
    slots = jnp.arange(stations, dtype=jnp.int32)[:, None]
    chosen = weights[:, slots, antenna_slot_index].astype(jnp.float32)

    def station_beam(index):
        volt = voltages[:, index].astype(jnp.float32)
        wsel = chosen[:, index]
        real_part = jnp.einsum("apc,apct->cpt", wsel[0], volt[0]) - jnp.einsum("apc,apct->cpt", wsel[1], volt[1])
        imag_part = jnp.einsum("apc,apct->cpt", wsel[0], volt[1]) + jnp.einsum("apc,apct->cpt", wsel[1], volt[0])
        return jnp.stack([real_part, imag_part], axis=1)

    stacked = lax.map(station_beam, jnp.arange(stations, dtype=jnp.int32))
    beams = jnp.transpose(stacked, (1, 2, 0, 3, 4)).astype(jnp.bfloat16)
    ordered = jnp.zeros_like(beams).at[:, :, station_order].set(beams)
    channels, _, _, polars, spectra = ordered.shape
    every_row = ordered.reshape(channels, 2, stations * polars, spectra)
    scale = 1.0 / spectra

    def correlate(block):
        real_in = block[0]
        imag_in = block[1]
        visibility_real = jnp.dot(real_in, real_in.T, preferred_element_type=jnp.float32) + jnp.dot(imag_in, imag_in.T, preferred_element_type=jnp.float32)
        imag_vis = jnp.dot(imag_in, real_in.T, preferred_element_type=jnp.float32) - jnp.dot(real_in, imag_in.T, preferred_element_type=jnp.float32)
        return jnp.stack([visibility_real * scale, imag_vis * scale], axis=0)

    return lax.map(correlate, every_row)
```

```python
import functools

import jax
import jax.numpy as jnp
from jax import lax
from jax.experimental import pallas as pl
from jax.experimental.pallas import tpu as pltpu
from jax.sharding import PartitionSpec as P

F32, BF16 = jnp.float32, jnp.bfloat16


def iota(shape, axis):
    return lax.broadcasted_iota(jnp.int32, shape, axis)


def dot(left, right):
    return jnp.dot(left, right, preferred_element_type=F32)


def beam_kernel(owners, me_ref, index_ref, w_ref, v_ref, keep_ref, send_ref, acc_ref, spread_ref):
    step = pl.program_id(0)
    _, stations, antennas, polars, channels, spectra = v_ref.shape
    numbers = w_ref.shape[-1]
    per_owner = channels // owners
    rows = 2 * channels
    me = me_ref[0]

    @pl.when(step == 0)
    def _():
        lanes = iota(spread_ref.shape, 1) // channels
        spread_ref[...] = jnp.where(lanes == iota(spread_ref.shape, 0), 1.0, 0.0).astype(BF16)

    def channel_of(shape):
        row = iota(shape, 0) % rows
        owner = (row // (2 * per_owner)) ^ me
        return owner * per_owner + row % per_owner

    shape = (2 * rows, rows)
    row = iota(shape, 0)
    half, part = row // rows, (row // per_owner) % 2
    source = (half ^ part) * channels + channel_of(shape)
    sign = jnp.where((half == 1) & (part == 0), -1.0, 1.0)
    pick = jnp.where(iota(shape, 1) == source, sign, 0.0).astype(BF16)
    lane_tile = min(128, antennas * channels)
    shape = (2 * rows, lane_tile)
    mask = iota(shape, 1) % channels == channel_of(shape)

    for s in range(stations):
        line = index_ref[pl.ds(step * stations + s, 1), :]
        chosen = jnp.where(iota((numbers, antennas), 0) == line, 1.0, 0.0).astype(BF16)
        for p in range(polars):
            both = jnp.concatenate([w_ref[0, s, p], w_ref[1, s, p]], axis=0)
            picked = dot(pick, both).astype(BF16)
            compact = dot(picked, chosen).astype(BF16)
            wide = dot(compact, spread_ref[...])
            left = jnp.concatenate(
                [
                    jnp.where(mask, wide[:, i : i + lane_tile], 0.0).astype(BF16)
                    for i in range(0, wide.shape[1], lane_tile)
                ],
                axis=1,
            )
            total = dot(left[:rows], v_ref[0, s, :, p].reshape(antennas * channels, spectra))
            total += dot(left[rows:], v_ref[1, s, :, p].reshape(antennas * channels, spectra))
            at = ((step * stations + s) * polars + p) * rows
            acc_ref[pl.ds(pl.multiple_of(at, rows), rows), :] = total

    @pl.when(step == pl.num_programs(0) - 1)
    def _():
        count = acc_ref.shape[0] // rows
        for r in range(rows):
            line = acc_ref[pl.ds(r, count, stride=rows), :]
            slot, inner = divmod(r, 2 * per_owner)
            target = send_ref if slot % 2 else keep_ref
            target[slot // 2, inner] = line.astype(target.dtype)


def beam(owners, me, index, weights, voltages, block):
    _, stations, antennas, polars, channels, spectra = voltages.shape
    numbers = weights.shape[-1]
    rows = 2 * channels
    half = (owners // 2, rows // owners, stations * polars, spectra)
    return pl.pallas_call(
        functools.partial(beam_kernel, owners),
        out_shape=(jax.ShapeDtypeStruct(half, F32), jax.ShapeDtypeStruct(half, F32)),
        grid_spec=pltpu.PrefetchScalarGridSpec(
            num_scalar_prefetch=1,
            grid=(stations // block,),
            in_specs=[
                pl.BlockSpec((stations, antennas), lambda i, m: (0, 0)),
                pl.BlockSpec((2, block, polars, channels, numbers), lambda i, m: (0, i, 0, 0, 0)),
                pl.BlockSpec((2, block, antennas, polars, channels, spectra), lambda i, m: (0, i, 0, 0, 0, 0)),
            ],
            out_specs=[pl.BlockSpec(half, lambda i, m: (0, 0, 0, 0))] * 2,
            scratch_shapes=[
                pltpu.VMEM((stations * polars * rows, spectra), F32),
                pltpu.VMEM((antennas, antennas * channels), BF16),
            ],
        ),
        compiler_params=pltpu.CompilerParams(dimension_semantics=("arbitrary",), vmem_limit_bytes=48 << 20),
        name="beam",
    )(me, index, weights, voltages)


def correlate_kernel(me_ref, order_ref, *refs):
    blocks, out_ref, row_ref = refs[:-2], refs[-2], refs[-1]
    groups = len(blocks)
    inner, local, spectra = blocks[0].shape
    channels = inner // 2
    total = groups * local
    stations = order_ref.shape[1]
    here = local * stations // total
    me = me_ref[0]
    polars = total // stations
    number = iota((total, stations), 0) // polars
    owns = jnp.where(order_ref[...] == number, 1.0, 0.0).astype(BF16)
    column = iota((stations, total), 1)
    slot = ((column // local) ^ me) * here + (column % local) // polars
    slots = jnp.where(iota((stations, total), 0) == slot, 1.0, 0.0).astype(BF16)
    same = iota((total, total), 0) % polars == iota((total, total), 1) % polars
    place = jnp.where(same, dot(owns, slots), 0.0).astype(BF16)
    scale = 1.0 / spectra
    for c in range(channels):
        real = jnp.concatenate([b[c] for b in blocks], axis=0)
        imag = jnp.concatenate([b[channels + c] for b in blocks], axis=0)
        both = jnp.concatenate([real, imag], axis=1)
        ordered = dot(place, both).astype(BF16)
        row_ref[...] = ordered
        mine = row_ref[pl.ds(pl.multiple_of(me * local, local), local), :]
        left = jnp.concatenate(
            [mine, jnp.concatenate([mine[:, spectra:], -mine[:, :spectra]], axis=1)], axis=0
        )
        vis = lax.dot_general(left, ordered, (((1,), (1,)), ((), ())), preferred_element_type=F32) * scale
        out_ref[c, 0] = vis[:local]
        out_ref[c, 1] = vis[local:]


def correlate(me, order, blocks):
    inner, local, spectra = blocks[0].shape
    total = len(blocks) * local
    shape = (inner // 2, 2, local, total)
    vmem = pl.BlockSpec(memory_space=pltpu.VMEM)
    return pl.pallas_call(
        correlate_kernel,
        out_shape=jax.ShapeDtypeStruct(shape, F32),
        in_specs=[pl.BlockSpec(memory_space=pltpu.SMEM), vmem] + [vmem] * len(blocks),
        out_specs=vmem,
        scratch_shapes=[pltpu.VMEM((total, 2 * spectra), BF16)],
        compiler_params=pltpu.CompilerParams(vmem_limit_bytes=48 << 20),
        name="correlate",
    )(me, order[None, :], *blocks)


def exchange(value, axis, size, bit):
    return lax.ppermute(value, axis, [(i, i ^ bit) for i in range(size)])


def body(groups, owners, voltages, weights, antenna_slot_index, station_order):
    group = lax.axis_index("sgroup").astype(jnp.int32)[None]
    tile = lax.axis_index("tile").astype(jnp.int32)[None]
    keep, send = beam(owners, tile, antenna_slot_index, jnp.transpose(weights, (0, 1, 3, 4, 2)), voltages, 1)
    total = keep + exchange(send, "tile", owners, 1)
    bit = 2
    while bit < owners:
        sent = exchange(total[1::2].astype(BF16), "tile", owners, bit)
        total = total[0::2] + sent.astype(F32)
        bit *= 2
    blocks = {0: total[0].astype(BF16)}
    bit = groups // 2
    while bit:
        blocks |= {i ^ bit: exchange(b, "sgroup", groups, bit) for i, b in blocks.items()}
        bit //= 2
    return correlate(group, station_order, [blocks[i] for i in range(groups)])


def solution(mesh):
    in_specs = (
        P(None, "sgroup", "tile", None, None, None),
        P(None, "sgroup", None, None, None),
        P("sgroup", "tile"),
        P(),
    )
    run = functools.partial(body, mesh.shape["sgroup"], mesh.shape["tile"])
    return jax.shard_map(run, mesh=mesh, in_specs=in_specs, out_specs=P("tile", None, "sgroup", None), check_vma=False)
```

```python
import functools

import jax
import jax.numpy as jnp
from jax import lax
from jax.experimental import pallas as pl
from jax.experimental.pallas import tpu as pltpu
from jax.sharding import PartitionSpec as P

F32, BF16 = jnp.float32, jnp.bfloat16


def iota(shape, axis):
    return lax.broadcasted_iota(jnp.int32, shape, axis)


def dot(left, right):
    return jnp.dot(left, right, preferred_element_type=F32)


def beam_kernel(owners, me_ref, index_hbm, w_hbm, v_hbm, keep_ref, send_ref, index_ref, w_ref, v_ref, left_ref, acc_ref, small_sem, v_sem):
    _, stations, antennas, polars, channels, spectra = v_ref.shape
    numbers = w_ref.shape[-1]
    per_owner = channels // owners
    rows = 2 * channels
    me = me_ref[0]

    copies = [pltpu.make_async_copy(index_hbm, index_ref, small_sem.at[0]), pltpu.make_async_copy(w_hbm, w_ref, small_sem.at[1])]
    arrivals = [pltpu.make_async_copy(v_hbm.at[:, s], v_ref.at[:, s], v_sem.at[s]) for s in range(stations)]
    for copy in copies + arrivals:
        copy.start()

    spread = jnp.where(iota((antennas, antennas * channels), 1) // channels == iota((antennas, antennas * channels), 0), 1.0, 0.0).astype(BF16)
    lane_tile = min(128, antennas * channels)
    mask = iota((rows, lane_tile), 1) % channels == iota((rows, lane_tile), 0) % channels
    number = iota((numbers, antennas), 0)
    for copy in copies:
        copy.wait()
    compact = []
    for s in range(stations):
        chosen = jnp.where(number == index_ref[s : s + 1, :], 1.0, 0.0).astype(BF16)
        lines = jnp.concatenate([w_ref[k, s, p] for p in range(polars) for k in range(2)], axis=0)
        compact.append(dot(lines, chosen).astype(BF16))
    for s in range(stations):
        wide = dot(compact[s], spread)
        for p in range(polars):
            for i in range(0, antennas * channels, lane_tile):
                part = wide[p * rows : (p + 1) * rows, i : i + lane_tile]
                left_ref[s, p, :, i : i + lane_tile] = jnp.where(mask, part, 0.0).astype(BF16)

    for s in range(stations):
        arrivals[s].wait()
        for p in range(polars):
            left = left_ref[s, p]
            real = dot(left, v_ref[0, s, :, p].reshape(antennas * channels, spectra))
            imag = dot(left, v_ref[1, s, :, p].reshape(antennas * channels, spectra))
            at = (s * polars + p) * rows
            acc_ref[at : at + channels, :] = real[:channels] - imag[channels:]
            acc_ref[at + channels : at + rows, :] = real[channels:] + imag[:channels]

    count = stations * polars
    for slot in range(owners):
        target = send_ref if slot % 2 else keep_ref
        first = (me ^ slot) * per_owner
        for part in range(2):
            for c in range(per_owner):
                line = acc_ref[pl.ds(first + part * channels + c, count, stride=rows), :]
                target[slot // 2, part * per_owner + c] = line.astype(target.dtype)


def beam(owners, me, index, weights, voltages):
    _, stations, antennas, polars, channels, spectra = voltages.shape
    rows = 2 * channels
    half = (owners // 2, rows // owners, stations * polars, spectra)
    hbm, vmem = pl.BlockSpec(memory_space=pltpu.HBM), pl.BlockSpec(memory_space=pltpu.VMEM)
    return pl.pallas_call(
        functools.partial(beam_kernel, owners),
        out_shape=(jax.ShapeDtypeStruct(half, F32), jax.ShapeDtypeStruct(half, F32)),
        in_specs=[pl.BlockSpec(memory_space=pltpu.SMEM), hbm, hbm, hbm],
        out_specs=[vmem, vmem],
        scratch_shapes=[
            pltpu.VMEM(index.shape, jnp.int32),
            pltpu.VMEM(weights.shape, BF16),
            pltpu.VMEM(voltages.shape, BF16),
            pltpu.VMEM((stations, polars, rows, antennas * channels), BF16),
            pltpu.VMEM((stations * polars * rows, spectra), F32),
            pltpu.SemaphoreType.DMA((2,)),
            pltpu.SemaphoreType.DMA((stations,)),
        ],
        compiler_params=pltpu.CompilerParams(vmem_limit_bytes=48 << 20),
        name="beam",
    )(me, index, weights, voltages)


def correlate_kernel(me_ref, order_ref, *refs):
    blocks, out_ref, row_ref = refs[:-2], refs[-2], refs[-1]
    groups = len(blocks)
    inner, local, spectra = blocks[0].shape
    channels = inner // 2
    total = groups * local
    stations = order_ref.shape[1]
    here = local * stations // total
    me = me_ref[0]
    polars = total // stations
    number = iota((total, stations), 0) // polars
    owns = jnp.where(order_ref[...] == number, 1.0, 0.0).astype(BF16)
    column = iota((stations, total), 1)
    slot = ((column // local) ^ me) * here + (column % local) // polars
    slots = jnp.where(iota((stations, total), 0) == slot, 1.0, 0.0).astype(BF16)
    same = iota((total, total), 0) % polars == iota((total, total), 1) % polars
    place = jnp.where(same, dot(owns, slots), 0.0).astype(BF16)
    scale = 1.0 / spectra
    for c in range(channels):
        real = jnp.concatenate([b[c] for b in blocks], axis=0)
        imag = jnp.concatenate([b[channels + c] for b in blocks], axis=0)
        both = jnp.concatenate([real, imag], axis=1)
        ordered = dot(place, both).astype(BF16)
        row_ref[...] = ordered
        mine = row_ref[pl.ds(pl.multiple_of(me * local, local), local), :]
        left = jnp.concatenate(
            [mine, jnp.concatenate([mine[:, spectra:], -mine[:, :spectra]], axis=1)], axis=0
        )
        vis = lax.dot_general(left, ordered, (((1,), (1,)), ((), ())), preferred_element_type=F32) * scale
        out_ref[c, 0] = vis[:local]
        out_ref[c, 1] = vis[local:]


def correlate(me, order, blocks):
    inner, local, spectra = blocks[0].shape
    total = len(blocks) * local
    shape = (inner // 2, 2, local, total)
    vmem = pl.BlockSpec(memory_space=pltpu.VMEM)
    return pl.pallas_call(
        correlate_kernel,
        out_shape=jax.ShapeDtypeStruct(shape, F32),
        in_specs=[pl.BlockSpec(memory_space=pltpu.SMEM), vmem] + [vmem] * len(blocks),
        out_specs=vmem,
        scratch_shapes=[pltpu.VMEM((total, 2 * spectra), BF16)],
        compiler_params=pltpu.CompilerParams(vmem_limit_bytes=48 << 20),
        name="correlate",
    )(me, order[None, :], *blocks)


def exchange(value, axis, size, bit):
    return lax.ppermute(value, axis, [(i, i ^ bit) for i in range(size)])


def body(groups, owners, voltages, weights, antenna_slot_index, station_order):
    group = lax.axis_index("sgroup").astype(jnp.int32)[None]
    tile = lax.axis_index("tile").astype(jnp.int32)[None]
    keep, send = beam(owners, tile, antenna_slot_index, jnp.transpose(weights, (0, 1, 3, 4, 2)), voltages)
    total = keep + exchange(send, "tile", owners, 1)
    bit = 2
    while bit < owners:
        sent = exchange(total[1::2].astype(BF16), "tile", owners, bit)
        total = total[0::2] + sent.astype(F32)
        bit *= 2
    blocks = {0: total[0].astype(BF16)}
    bit = groups // 2
    while bit:
        blocks |= {i ^ bit: exchange(b, "sgroup", groups, bit) for i, b in blocks.items()}
        bit //= 2
    return correlate(group, station_order, [blocks[i] for i in range(groups)])


def solution(mesh):
    in_specs = (
        P(None, "sgroup", "tile", None, None, None),
        P(None, "sgroup", None, None, None),
        P("sgroup", "tile"),
        P(),
    )
    run = functools.partial(body, mesh.shape["sgroup"], mesh.shape["tile"])
    return jax.shard_map(run, mesh=mesh, in_specs=in_specs, out_specs=P("tile", None, "sgroup", None), check_vma=False)
```

```python
import functools

import jax
import jax.numpy as jnp
from jax import lax
from jax.experimental import pallas as pl
from jax.experimental.pallas import tpu as pltpu
from jax.sharding import PartitionSpec as P

F32, BF16 = jnp.float32, jnp.bfloat16


def iota(shape, axis):
    return lax.broadcasted_iota(jnp.int32, shape, axis)


def dot(left, right):
    return jnp.dot(left, right, preferred_element_type=F32)


def beam_kernel(owners, me_ref, index_hbm, w_hbm, v_hbm, keep_ref, send_ref, index_ref, w_ref, v_ref, left_ref, acc_ref, small_sem, v_sem):
    _, stations, antennas, polars, channels, spectra = v_ref.shape
    numbers = w_ref.shape[-1]
    per_owner = channels // owners
    rows = 2 * channels
    me = me_ref[0]

    copies = [pltpu.make_async_copy(index_hbm, index_ref, small_sem.at[0]), pltpu.make_async_copy(w_hbm, w_ref, small_sem.at[1])]
    arrivals = [pltpu.make_async_copy(v_hbm.at[:, s], v_ref.at[:, s], v_sem.at[s]) for s in range(stations)]
    early = 2
    for copy in copies + arrivals[:early]:
        copy.start()

    spread = jnp.where(iota((antennas, antennas * channels), 1) // channels == iota((antennas, antennas * channels), 0), 1.0, 0.0).astype(BF16)
    lane_tile = min(128, antennas * channels)
    mask = iota((rows, lane_tile), 1) % channels == iota((rows, lane_tile), 0) % channels
    number = iota((numbers, antennas), 0)
    for copy in copies:
        copy.wait()
    for copy in arrivals[early:]:
        copy.start()
    compact = []
    for s in range(stations):
        chosen = jnp.where(number == index_ref[s : s + 1, :], 1.0, 0.0).astype(BF16)
        lines = jnp.concatenate([w_ref[k, s, p] for p in range(polars) for k in range(2)], axis=0)
        compact.append(dot(lines, chosen).astype(BF16))
    for s in range(stations):
        wide = dot(compact[s], spread)
        for p in range(polars):
            for i in range(0, antennas * channels, lane_tile):
                part = wide[p * rows : (p + 1) * rows, i : i + lane_tile]
                left_ref[s, p, :, i : i + lane_tile] = jnp.where(mask, part, 0.0).astype(BF16)

    for s in range(stations):
        arrivals[s].wait()
        for p in range(polars):
            left = left_ref[s, p]
            real = dot(left, v_ref[0, s, :, p].reshape(antennas * channels, spectra))
            imag = dot(left, v_ref[1, s, :, p].reshape(antennas * channels, spectra))
            at = (s * polars + p) * rows
            acc_ref[at : at + channels, :] = real[:channels] - imag[channels:]
            acc_ref[at + channels : at + rows, :] = real[channels:] + imag[:channels]

    count = stations * polars
    for slot in range(owners):
        target = send_ref if slot % 2 else keep_ref
        first = (me ^ slot) * per_owner
        for part in range(2):
            for c in range(per_owner):
                line = acc_ref[pl.ds(first + part * channels + c, count, stride=rows), :]
                target[slot // 2, part * per_owner + c] = line.astype(target.dtype)


def beam(owners, me, index, weights, voltages):
    _, stations, antennas, polars, channels, spectra = voltages.shape
    rows = 2 * channels
    half = (owners // 2, rows // owners, stations * polars, spectra)
    hbm, vmem = pl.BlockSpec(memory_space=pltpu.HBM), pl.BlockSpec(memory_space=pltpu.VMEM)
    return pl.pallas_call(
        functools.partial(beam_kernel, owners),
        out_shape=(jax.ShapeDtypeStruct(half, F32), jax.ShapeDtypeStruct(half, F32)),
        in_specs=[pl.BlockSpec(memory_space=pltpu.SMEM), hbm, hbm, hbm],
        out_specs=[vmem, vmem],
        scratch_shapes=[
            pltpu.VMEM(index.shape, jnp.int32),
            pltpu.VMEM(weights.shape, BF16),
            pltpu.VMEM(voltages.shape, BF16),
            pltpu.VMEM((stations, polars, rows, antennas * channels), BF16),
            pltpu.VMEM((stations * polars * rows, spectra), F32),
            pltpu.SemaphoreType.DMA((2,)),
            pltpu.SemaphoreType.DMA((stations,)),
        ],
        compiler_params=pltpu.CompilerParams(vmem_limit_bytes=48 << 20),
        name="beam",
    )(me, *(pltpu.with_memory_space_constraint(a, pltpu.HBM) for a in (index, weights, voltages)))


def correlate_kernel(me_ref, order_ref, *refs):
    blocks, out_ref, row_ref = refs[:-2], refs[-2], refs[-1]
    groups = len(blocks)
    inner, local, spectra = blocks[0].shape
    channels = inner // 2
    total = groups * local
    stations = order_ref.shape[1]
    here = local * stations // total
    me = me_ref[0]
    polars = total // stations
    number = iota((total, stations), 0) // polars
    owns = jnp.where(order_ref[...] == number, 1.0, 0.0).astype(BF16)
    column = iota((stations, total), 1)
    slot = ((column // local) ^ me) * here + (column % local) // polars
    slots = jnp.where(iota((stations, total), 0) == slot, 1.0, 0.0).astype(BF16)
    same = iota((total, total), 0) % polars == iota((total, total), 1) % polars
    place = jnp.where(same, dot(owns, slots), 0.0).astype(BF16)
    scale = 1.0 / spectra
    for c in range(channels):
        real = jnp.concatenate([b[c] for b in blocks], axis=0)
        imag = jnp.concatenate([b[channels + c] for b in blocks], axis=0)
        both = jnp.concatenate([real, imag], axis=1)
        ordered = dot(place, both).astype(BF16)
        row_ref[...] = ordered
        mine = row_ref[pl.ds(pl.multiple_of(me * local, local), local), :]
        left = jnp.concatenate(
            [mine, jnp.concatenate([mine[:, spectra:], -mine[:, :spectra]], axis=1)], axis=0
        )
        vis = lax.dot_general(left, ordered, (((1,), (1,)), ((), ())), preferred_element_type=F32) * scale
        out_ref[c, 0] = vis[:local]
        out_ref[c, 1] = vis[local:]


def correlate(me, order, blocks):
    inner, local, spectra = blocks[0].shape
    total = len(blocks) * local
    shape = (inner // 2, 2, local, total)
    vmem = pl.BlockSpec(memory_space=pltpu.VMEM)
    return pl.pallas_call(
        correlate_kernel,
        out_shape=jax.ShapeDtypeStruct(shape, F32),
        in_specs=[pl.BlockSpec(memory_space=pltpu.SMEM), vmem] + [vmem] * len(blocks),
        out_specs=vmem,
        scratch_shapes=[pltpu.VMEM((total, 2 * spectra), BF16)],
        compiler_params=pltpu.CompilerParams(vmem_limit_bytes=48 << 20),
        name="correlate",
    )(me, order[None, :], *blocks)


def exchange(value, axis, size, bit):
    return lax.ppermute(value, axis, [(i, i ^ bit) for i in range(size)])


def body(groups, owners, voltages, weights, antenna_slot_index, station_order):
    group = lax.axis_index("sgroup").astype(jnp.int32)[None]
    tile = lax.axis_index("tile").astype(jnp.int32)[None]
    keep, send = beam(owners, tile, antenna_slot_index, jnp.transpose(weights, (0, 1, 3, 4, 2)), voltages)
    total = keep + exchange(send, "tile", owners, 1)
    bit = 2
    while bit < owners:
        sent = exchange(total[1::2].astype(BF16), "tile", owners, bit)
        total = total[0::2] + sent.astype(F32)
        bit *= 2
    blocks = {0: total[0].astype(BF16)}
    far = groups // 2
    blocks[far] = exchange(blocks[0], "sgroup", groups, far)
    for i in range(1, far):
        blocks[i] = exchange(blocks[0], "sgroup", groups, i)
    for i in range(far - 1, 0, -1):
        blocks[far ^ i] = exchange(blocks[far], "sgroup", groups, i)
    return correlate(group, station_order, [blocks[i] for i in range(groups)])


def solution(mesh):
    in_specs = (
        P(None, "sgroup", "tile", None, None, None),
        P(None, "sgroup", None, None, None),
        P("sgroup", "tile"),
        P(),
    )
    run = functools.partial(body, mesh.shape["sgroup"], mesh.shape["tile"])
    return jax.shard_map(run, mesh=mesh, in_specs=in_specs, out_specs=P("tile", None, "sgroup", None), check_vma=False)
```

```python
import functools

import jax
import jax.numpy as jnp
from jax import lax
from jax.experimental import pallas as pl
from jax.experimental.pallas import tpu as pltpu
from jax.sharding import PartitionSpec as P


F32, BF16 = jnp.float32, jnp.bfloat16


def iota(shape, axis):
    return lax.broadcasted_iota(jnp.int32, shape, axis)


def dot(left, right):
    return jnp.dot(left, right, preferred_element_type=F32)


def beam_kernel(owners, me_ref, index_hbm, w_hbm, v_hbm, keep_ref, send_ref, index_ref, w_ref, v_ref, left_ref, acc_ref, small_sem, v_sem):
    _, stations, antennas, polars, channels, spectra = v_ref.shape
    numbers = w_ref.shape[-1]
    per_owner = channels // owners
    rows = 2 * channels
    me = me_ref[0]
    together = 2 - stations % 2

    copies = [pltpu.make_async_copy(index_hbm, index_ref, small_sem.at[0]), pltpu.make_async_copy(w_hbm, w_ref, small_sem.at[1])]
    arrivals = [
        pltpu.make_async_copy(v_hbm.at[:, s : s + together], v_ref.at[:, s : s + together], v_sem.at[s])
        for s in range(0, stations, together)
    ]
    for copy in copies:
        copy.start(priority=0)
    for copy in arrivals:
        copy.start(priority=1)

    spread = jnp.where(iota((antennas, antennas * channels), 1) // channels == iota((antennas, antennas * channels), 0), 1.0, 0.0).astype(BF16)
    lane_tile = min(128, antennas * channels)
    mask = iota((rows, lane_tile), 1) % channels == iota((rows, lane_tile), 0) % channels
    number = iota((numbers, antennas), 0)
    for copy in copies:
        copy.wait()
    compact = []
    for s in range(stations):
        chosen = jnp.where(number == index_ref[s : s + 1, :], 1.0, 0.0).astype(BF16)
        lines = jnp.concatenate([w_ref[k, s, p] for p in range(polars) for k in range(2)], axis=0)
        compact.append(dot(lines, chosen).astype(BF16))
    for s in range(stations):
        wide = dot(compact[s], spread)
        for p in range(polars):
            for i in range(0, antennas * channels, lane_tile):
                part = wide[p * rows : (p + 1) * rows, i : i + lane_tile]
                left_ref[s, p, :, i : i + lane_tile] = jnp.where(mask, part, 0.0).astype(BF16)

    for s in range(stations):
        if s % together == 0:
            arrivals[s // together].wait()
        for p in range(polars):
            left = left_ref[s, p]
            real = dot(left, v_ref[0, s, :, p].reshape(antennas * channels, spectra))
            imag = dot(left, v_ref[1, s, :, p].reshape(antennas * channels, spectra))
            at = (s * polars + p) * rows
            acc_ref[at : at + channels, :] = real[:channels] - imag[channels:]
            acc_ref[at + channels : at + rows, :] = real[channels:] + imag[:channels]

    count = stations * polars
    for slot in range(owners):
        target = send_ref if slot % 2 else keep_ref
        first = (me ^ slot) * per_owner
        for part in range(2):
            for c in range(per_owner):
                line = acc_ref[pl.ds(first + part * channels + c, count, stride=rows), :]
                target[slot // 2, part * per_owner + c] = line.astype(target.dtype)


def beam(owners, me, index, weights, voltages):
    _, stations, antennas, polars, channels, spectra = voltages.shape
    rows = 2 * channels
    half = (owners // 2, rows // owners, stations * polars, spectra)
    hbm, vmem = pl.BlockSpec(memory_space=pltpu.HBM), pl.BlockSpec(memory_space=pltpu.VMEM)
    return pl.pallas_call(
        functools.partial(beam_kernel, owners),
        out_shape=(jax.ShapeDtypeStruct(half, F32), jax.ShapeDtypeStruct(half, F32)),
        in_specs=[pl.BlockSpec(memory_space=pltpu.SMEM), hbm, hbm, hbm],
        out_specs=[vmem, vmem],
        scratch_shapes=[
            pltpu.VMEM(index.shape, jnp.int32),
            pltpu.VMEM(weights.shape, BF16),
            pltpu.VMEM(voltages.shape, BF16),
            pltpu.VMEM((stations, polars, rows, antennas * channels), BF16),
            pltpu.VMEM((stations * polars * rows, spectra), F32),
            pltpu.SemaphoreType.DMA((2,)),
            pltpu.SemaphoreType.DMA((stations,)),
        ],
        compiler_params=pltpu.CompilerParams(vmem_limit_bytes=48 << 20),
        name="beam",
    )(me, *(pltpu.with_memory_space_constraint(a, pltpu.HBM) for a in (index, weights, voltages)))


def correlate_kernel(me_ref, order_ref, *refs):
    blocks, out_ref, row_ref = refs[:-2], refs[-2], refs[-1]
    groups = len(blocks)
    inner, local, spectra = blocks[0].shape
    channels = inner // 2
    total = groups * local
    stations = order_ref.shape[1]
    here = local * stations // total
    me = me_ref[0]
    polars = total // stations
    number = iota((total, stations), 0) // polars
    owns = jnp.where(order_ref[...] == number, 1.0, 0.0).astype(BF16)
    column = iota((stations, total), 1)
    slot = ((column // local) ^ me) * here + (column % local) // polars
    slots = jnp.where(iota((stations, total), 0) == slot, 1.0, 0.0).astype(BF16)
    same = iota((total, total), 0) % polars == iota((total, total), 1) % polars
    place = jnp.where(same, dot(owns, slots), 0.0).astype(BF16)
    scale = 1.0 / spectra
    for c in range(channels):
        real = jnp.concatenate([b[c] for b in blocks], axis=0)
        imag = jnp.concatenate([b[channels + c] for b in blocks], axis=0)
        both = jnp.concatenate([real, imag], axis=1)
        ordered = dot(place, both).astype(BF16)
        row_ref[...] = ordered
        mine = row_ref[pl.ds(pl.multiple_of(me * local, local), local), :]
        left = jnp.concatenate(
            [mine, jnp.concatenate([mine[:, spectra:], -mine[:, :spectra]], axis=1)], axis=0
        )
        vis = lax.dot_general(left, ordered, (((1,), (1,)), ((), ())), preferred_element_type=F32) * scale
        out_ref[c, 0] = vis[:local]
        out_ref[c, 1] = vis[local:]


def correlate(me, order, blocks):
    inner, local, spectra = blocks[0].shape
    total = len(blocks) * local
    shape = (inner // 2, 2, local, total)
    vmem = pl.BlockSpec(memory_space=pltpu.VMEM)
    return pl.pallas_call(
        correlate_kernel,
        out_shape=jax.ShapeDtypeStruct(shape, F32),
        in_specs=[pl.BlockSpec(memory_space=pltpu.SMEM), vmem] + [vmem] * len(blocks),
        out_specs=vmem,
        scratch_shapes=[pltpu.VMEM((total, 2 * spectra), BF16)],
        compiler_params=pltpu.CompilerParams(vmem_limit_bytes=48 << 20),
        name="correlate",
    )(me, order[None, :], *blocks)


def body(groups, owners, voltages, weights, antenna_slot_index, station_order):
    group, tile = lax.axis_index("sgroup").astype(jnp.int32), lax.axis_index("tile").astype(jnp.int32)
    far = groups // 2

    def exchange(value, axis, size, bit):
        return lax.ppermute(value, axis, [(i, i ^ bit) for i in range(size)])

    def share(value, bit):
        return exchange(value, "sgroup", groups, bit)

    keep, send = beam(owners, tile[None], antenna_slot_index, jnp.transpose(weights, (0, 1, 3, 4, 2)), voltages)
    total = keep + exchange(send, "tile", owners, 1)
    bit = 2
    while bit < owners:
        sent = exchange(total[1::2].astype(BF16), "tile", owners, bit)
        total = total[0::2] + sent.astype(F32)
        bit *= 2
    own = total[0].astype(BF16)
    blocks = {0: own, far: share(own, far)}
    for i in range(far - 2, 0, -1):
        blocks[i] = share(own, i)
    both = share(jnp.stack([own, blocks[far]]), far - 1)
    blocks[far - 1], blocks[far + far - 1] = both[0], both[1]
    for i in range(1, far - 1):
        blocks[far + i] = share(blocks[far], i)
    return correlate(group[None], station_order, [blocks[i] for i in range(groups)])


def solution(mesh):
    groups = mesh.shape["sgroup"]
    in_specs = (
        P(None, "sgroup", "tile", None, None, None),
        P(None, "sgroup", None, None, None),
        P("sgroup", "tile"),
        P(),
    )
    run = functools.partial(body, groups, mesh.shape["tile"])
    return jax.shard_map(run, mesh=mesh, in_specs=in_specs, out_specs=P("tile", None, "sgroup", None), check_vma=False)
```

```python
import functools

import jax
import jax.numpy as jnp
from jax import lax
from jax.experimental import pallas as pl
from jax.experimental.pallas import tpu as pltpu
from jax.sharding import PartitionSpec as P


F32, BF16 = jnp.float32, jnp.bfloat16


def iota(shape, axis):
    return lax.broadcasted_iota(jnp.int32, shape, axis)


def dot(left, right):
    return jnp.dot(left, right, preferred_element_type=F32)


def beam_kernel(owners, me_ref, index_hbm, w_hbm, v_hbm, keep_ref, send_ref, index_ref, w_ref, v_ref, left_ref, acc_ref, small_sem, v_sem):
    _, stations, antennas, polars, channels, spectra = v_ref.shape
    numbers = w_ref.shape[-1]
    per_owner = channels // owners
    rows = 2 * channels
    me = me_ref[0]
    copies = [pltpu.make_async_copy(index_hbm, index_ref, small_sem.at[0]), pltpu.make_async_copy(w_hbm, w_ref, small_sem.at[1])]
    spans = [(s, min(s + 2, stations)) for s in range(0, stations - 2, 2)] + [(s, s + 1) for s in range(max(stations - 2, 0), stations)]
    arrivals = {a: pltpu.make_async_copy(v_hbm.at[:, a:b], v_ref.at[:, a:b], v_sem.at[a]) for a, b in spans}
    for copy in copies:
        copy.start(priority=0)
    for copy in arrivals.values():
        copy.start(priority=1)

    spread = jnp.where(iota((antennas, antennas * channels), 1) // channels == iota((antennas, antennas * channels), 0), 1.0, 0.0).astype(BF16)
    lane_tile = min(128, antennas * channels)
    mask = iota((rows, lane_tile), 1) % channels == iota((rows, lane_tile), 0) % channels
    number = iota((numbers, antennas), 0)
    for copy in copies:
        copy.wait()
    compact = []
    for s in range(stations):
        chosen = jnp.where(number == index_ref[s : s + 1, :], 1.0, 0.0).astype(BF16)
        lines = jnp.concatenate([w_ref[k, s, p] for p in range(polars) for k in range(2)], axis=0)
        compact.append(dot(lines, chosen).astype(BF16))
    for s in range(stations):
        wide = dot(compact[s], spread)
        for p in range(polars):
            for i in range(0, antennas * channels, lane_tile):
                part = wide[p * rows : (p + 1) * rows, i : i + lane_tile]
                left_ref[s, p, :, i : i + lane_tile] = jnp.where(mask, part, 0.0).astype(BF16)

    def order_rows(stop, size):
        for slot in range(owners):
            target = send_ref if slot % 2 else keep_ref
            first = (stop - size) * polars * rows + (me ^ slot) * per_owner
            for part in range(2):
                for c in range(per_owner):
                    line = acc_ref[pl.ds(first + part * channels + c, size * polars, stride=rows), :]
                    target[slot // 2, part * per_owner + c, (stop - size) * polars : stop * polars] = line

    batch = 4 if stations % 4 == 0 else stations
    for s in range(stations):
        if s in arrivals:
            arrivals[s].wait()
        for p in range(polars):
            left = left_ref[s, p]
            real = dot(left, v_ref[0, s, :, p].reshape(antennas * channels, spectra))
            imag = dot(left, v_ref[1, s, :, p].reshape(antennas * channels, spectra))
            at = (s * polars + p) * rows
            acc_ref[at : at + channels, :] = real[:channels] - imag[channels:]
            acc_ref[at + channels : at + rows, :] = real[channels:] + imag[:channels]
        if (s + 1) % batch == 0:
            order_rows(s + 1, batch)


def beam(owners, me, index, weights, voltages):
    _, stations, antennas, polars, channels, spectra = voltages.shape
    rows = 2 * channels
    half = (owners // 2, rows // owners, stations * polars, spectra)
    hbm, vmem = pl.BlockSpec(memory_space=pltpu.HBM), pl.BlockSpec(memory_space=pltpu.VMEM)
    return pl.pallas_call(
        functools.partial(beam_kernel, owners),
        out_shape=(jax.ShapeDtypeStruct(half, F32), jax.ShapeDtypeStruct(half, F32)),
        in_specs=[pl.BlockSpec(memory_space=pltpu.SMEM), hbm, hbm, hbm],
        out_specs=[vmem, vmem],
        scratch_shapes=[
            pltpu.VMEM(index.shape, jnp.int32),
            pltpu.VMEM(weights.shape, BF16),
            pltpu.VMEM(voltages.shape, BF16),
            pltpu.VMEM((stations, polars, rows, antennas * channels), BF16),
            pltpu.VMEM((stations * polars * rows, spectra), F32),
            pltpu.SemaphoreType.DMA((2,)),
            pltpu.SemaphoreType.DMA((stations,)),
        ],
        compiler_params=pltpu.CompilerParams(vmem_limit_bytes=48 << 20),
        name="beam",
    )(me, *(pltpu.with_memory_space_constraint(a, pltpu.HBM) for a in (index, weights, voltages)))


def place_kernel(local, polars, me_ref, order_ref, place_ref):
    total, stations = place_ref.shape[0], order_ref.shape[1]
    owns = jnp.where(order_ref[...] == iota((total, stations), 0) // polars, 1.0, 0.0).astype(BF16)
    column = iota((stations, total), 1)
    slot = ((column // local) ^ me_ref[0]) * (local // polars) + (column % local) // polars
    slots = jnp.where(iota((stations, total), 0) == slot, 1.0, 0.0).astype(BF16)
    same = iota((total, total), 0) % polars == iota((total, total), 1) % polars
    place_ref[...] = jnp.where(same, dot(owns, slots), 0.0).astype(BF16)


def placement(me, order, polars, local):
    vmem = pl.BlockSpec(memory_space=pltpu.VMEM)
    total = order.shape[0] * polars
    return pl.pallas_call(
        functools.partial(place_kernel, local, polars),
        out_shape=jax.ShapeDtypeStruct((total, total), BF16),
        in_specs=[pl.BlockSpec(memory_space=pltpu.SMEM), vmem],
        out_specs=vmem,
        compiler_params=pltpu.CompilerParams(vmem_limit_bytes=48 << 20),
        name="place",
    )(me, order[None, :])


def correlate_kernel(me_ref, place_ref, *refs):
    blocks, (out_hbm, row_ref, out_ref, sem) = refs[:-4], refs[-4:]
    inner, local, spectra = blocks[0].shape
    channels = inner // 2
    me, place = me_ref[0], place_ref[...]
    scale = 1.0 / spectra
    for c in range(channels):
        real = jnp.concatenate([b[c] for b in blocks], axis=0)
        imag = jnp.concatenate([b[channels + c] for b in blocks], axis=0)
        row_ref[c] = dot(place, jnp.concatenate([real, imag], axis=1)).astype(BF16)
    rows, copies = pl.ds(pl.multiple_of(me * local, local), local), []
    for c in range(channels):
        mine = row_ref[c, rows, :]
        left = jnp.concatenate(
            [mine, jnp.concatenate([mine[:, spectra:], -mine[:, :spectra]], axis=1)], axis=0
        )
        vis = lax.dot_general(left, row_ref[c], (((1,), (1,)), ((), ())), preferred_element_type=F32) * scale
        out_ref[c, 0] = vis[:local]
        out_ref[c, 1] = vis[local:]
        copies.append(pltpu.make_async_copy(out_ref.at[c], out_hbm.at[c], sem.at[c]))
        copies[-1].start()
    for copy in copies:
        copy.wait()


def correlate(me, place, blocks):
    inner, local, spectra = blocks[0].shape
    total = len(blocks) * local
    shape = (inner // 2, 2, local, total)
    vmem = pl.BlockSpec(memory_space=pltpu.VMEM)
    return pl.pallas_call(
        correlate_kernel,
        out_shape=jax.ShapeDtypeStruct(shape, F32),
        in_specs=[pl.BlockSpec(memory_space=pltpu.SMEM), vmem] + [vmem] * len(blocks),
        out_specs=pl.BlockSpec(memory_space=pltpu.HBM),
        scratch_shapes=[
            pltpu.VMEM((inner // 2, total, 2 * spectra), BF16),
            pltpu.VMEM(shape, F32),
            pltpu.SemaphoreType.DMA((inner // 2,)),
        ],
        compiler_params=pltpu.CompilerParams(vmem_limit_bytes=48 << 20),
        name="correlate",
    )(me, place, *blocks)


def body(groups, owners, voltages, weights, antenna_slot_index, station_order):
    group, tile = lax.axis_index("sgroup").astype(jnp.int32), lax.axis_index("tile").astype(jnp.int32)
    far = groups // 2

    def exchange(value, axis, size, bit):
        return lax.ppermute(value, axis, [(i, i ^ bit) for i in range(size)])

    def share(value, bit):
        return exchange(value, "sgroup", groups, bit)

    keep, send = beam(owners, tile[None], antenna_slot_index, jnp.transpose(weights, (0, 1, 3, 4, 2)), voltages)
    total = keep + exchange(send, "tile", owners, 1)
    bit = 2
    while bit < owners:
        sent = exchange(total[1::2].astype(BF16), "tile", owners, bit)
        total = total[0::2] + sent.astype(F32)
        bit *= 2
    own = total[0].astype(BF16)
    blocks = {0: own, far: share(own, far)}
    for i in range(far - 2, 0, -1):
        blocks[i] = share(own, i)
    both = share(jnp.stack([own, blocks[far]]), far - 1)
    blocks[far - 1], blocks[far + far - 1] = both[0], both[1]
    for i in range(1, far - 1):
        blocks[far + i] = share(blocks[far], i)
    place = placement(group[None], station_order, voltages.shape[3], own.shape[1])
    return correlate(group[None], place, [blocks[i] for i in range(groups)])


def solution(mesh):
    groups = mesh.shape["sgroup"]
    in_specs = (
        P(None, "sgroup", "tile", None, None, None),
        P(None, "sgroup", None, None, None),
        P("sgroup", "tile"),
        P(),
    )
    run = functools.partial(body, groups, mesh.shape["tile"])
    return jax.shard_map(run, mesh=mesh, in_specs=in_specs, out_specs=P("tile", None, "sgroup", None), check_vma=False)
```

```python
import functools

import jax
import jax.numpy as jnp
from jax import lax
from jax.experimental import pallas as pl
from jax.experimental.pallas import tpu as pltpu
from jax.sharding import PartitionSpec as P


F32, BF16 = jnp.float32, jnp.bfloat16


def iota(shape, axis):
    return lax.broadcasted_iota(jnp.int32, shape, axis)


def dot(left, right):
    return jnp.dot(left, right, preferred_element_type=F32)


def beam_kernel(owners, me_ref, index_hbm, w_hbm, v_hbm, keep_ref, send_ref, index_ref, w_ref, v_ref, left_ref, acc_ref, small_sem, v_sem):
    _, stations, antennas, polars, channels, spectra = v_ref.shape
    numbers = w_ref.shape[-1]
    per_owner = channels // owners
    rows = 2 * channels
    me = me_ref[0]
    copies = [pltpu.make_async_copy(index_hbm, index_ref, small_sem.at[0]), pltpu.make_async_copy(w_hbm, w_ref, small_sem.at[1])]
    spans = [(s, min(s + 2, stations)) for s in range(0, stations - 2, 2)] + [(s, s + 1) for s in range(max(stations - 2, 0), stations)]
    arrivals = {a: pltpu.make_async_copy(v_hbm.at[:, a:b], v_ref.at[:, a:b], v_sem.at[a]) for a, b in spans}
    for copy in copies:
        copy.start(priority=0)
    for copy in arrivals.values():
        copy.start(priority=1)

    spread = jnp.where(iota((antennas, antennas * channels), 1) // channels == iota((antennas, antennas * channels), 0), 1.0, 0.0).astype(BF16)
    lane_tile = min(128, antennas * channels)
    mask = iota((rows, lane_tile), 1) % channels == iota((rows, lane_tile), 0) % channels
    number = iota((numbers, antennas), 0)
    for copy in copies:
        copy.wait()
    compact = []
    for s in range(stations):
        chosen = jnp.where(number == index_ref[s : s + 1, :], 1.0, 0.0).astype(BF16)
        lines = jnp.concatenate([w_ref[k, s, p] for p in range(polars) for k in range(2)], axis=0)
        compact.append(dot(lines, chosen).astype(BF16))
    for s in range(stations):
        wide = dot(compact[s], spread)
        for p in range(polars):
            for i in range(0, antennas * channels, lane_tile):
                part = wide[p * rows : (p + 1) * rows, i : i + lane_tile]
                left_ref[s, p, :, i : i + lane_tile] = jnp.where(mask, part, 0.0).astype(BF16)

    def order_rows(stop, size):
        for slot in range(owners):
            target = send_ref if slot % 2 else keep_ref
            first = (stop - size) * polars * rows + (me ^ slot) * per_owner
            for part in range(2):
                for c in range(per_owner):
                    line = acc_ref[pl.ds(first + part * channels + c, size * polars, stride=rows), :]
                    target[slot // 2, part * per_owner + c, (stop - size) * polars : stop * polars] = line.astype(target.dtype)

    batch = 4 if stations % 4 == 0 else stations
    for s in range(stations):
        if s in arrivals:
            arrivals[s].wait()
        for p in range(polars):
            left = left_ref[s, p]
            real = dot(left, v_ref[0, s, :, p].reshape(antennas * channels, spectra))
            imag = dot(left, v_ref[1, s, :, p].reshape(antennas * channels, spectra))
            at = (s * polars + p) * rows
            acc_ref[at : at + channels, :] = real[:channels] - imag[channels:]
            acc_ref[at + channels : at + rows, :] = real[channels:] + imag[:channels]
        if (s + 1) % batch == 0:
            order_rows(s + 1, batch)


def beam(owners, me, index, weights, voltages):
    _, stations, antennas, polars, channels, spectra = voltages.shape
    rows = 2 * channels
    half = (owners // 2, rows // owners, stations * polars, spectra)
    hbm, vmem = pl.BlockSpec(memory_space=pltpu.HBM), pl.BlockSpec(memory_space=pltpu.VMEM)
    return pl.pallas_call(
        functools.partial(beam_kernel, owners),
        out_shape=(jax.ShapeDtypeStruct(half, F32), jax.ShapeDtypeStruct(half, BF16)),
        in_specs=[pl.BlockSpec(memory_space=pltpu.SMEM), hbm, hbm, hbm],
        out_specs=[vmem, vmem],
        scratch_shapes=[
            pltpu.VMEM(index.shape, jnp.int32),
            pltpu.VMEM(weights.shape, BF16),
            pltpu.VMEM(voltages.shape, BF16),
            pltpu.VMEM((stations, polars, rows, antennas * channels), BF16),
            pltpu.VMEM((stations * polars * rows, spectra), F32),
            pltpu.SemaphoreType.DMA((2,)),
            pltpu.SemaphoreType.DMA((stations,)),
        ],
        compiler_params=pltpu.CompilerParams(vmem_limit_bytes=48 << 20),
        name="beam",
    )(me, *(pltpu.with_memory_space_constraint(a, pltpu.HBM) for a in (index, weights, voltages)))


def place_kernel(local, polars, me_ref, order_ref, place_ref):
    total, stations = place_ref.shape[0], order_ref.shape[1]
    owns = jnp.where(order_ref[...] == iota((total, stations), 0) // polars, 1.0, 0.0).astype(BF16)
    column = iota((stations, total), 1)
    slot = ((column // local) ^ me_ref[0]) * (local // polars) + (column % local) // polars
    slots = jnp.where(iota((stations, total), 0) == slot, 1.0, 0.0).astype(BF16)
    same = iota((total, total), 0) % polars == iota((total, total), 1) % polars
    place_ref[...] = jnp.where(same, dot(owns, slots), 0.0).astype(BF16)


def placement(me, order, polars, local):
    vmem = pl.BlockSpec(memory_space=pltpu.VMEM)
    total = order.shape[0] * polars
    return pl.pallas_call(
        functools.partial(place_kernel, local, polars),
        out_shape=jax.ShapeDtypeStruct((total, total), BF16),
        in_specs=[pl.BlockSpec(memory_space=pltpu.SMEM), vmem],
        out_specs=vmem,
        compiler_params=pltpu.CompilerParams(vmem_limit_bytes=48 << 20),
        name="place",
    )(me, order[None, :])


def correlate_kernel(me_ref, place_ref, *refs):
    blocks, (out_hbm, row_ref, out_ref, sem) = refs[:-4], refs[-4:]
    inner, local, spectra = blocks[0].shape
    channels = inner // 2
    me, place = me_ref[0], place_ref[...]
    scale = 1.0 / spectra
    for c in range(channels):
        real = jnp.concatenate([b[c] for b in blocks], axis=0)
        imag = jnp.concatenate([b[channels + c] for b in blocks], axis=0)
        row_ref[c] = dot(place, jnp.concatenate([real, imag], axis=1)).astype(BF16)
    rows, copies = pl.ds(pl.multiple_of(me * local, local), local), []
    for c in range(channels):
        mine = row_ref[c, rows, :]
        left = jnp.concatenate(
            [mine, jnp.concatenate([mine[:, spectra:], -mine[:, :spectra]], axis=1)], axis=0
        )
        vis = lax.dot_general(left, row_ref[c], (((1,), (1,)), ((), ())), preferred_element_type=F32) * scale
        out_ref[c, 0] = vis[:local]
        out_ref[c, 1] = vis[local:]
        copies.append(pltpu.make_async_copy(out_ref.at[c], out_hbm.at[c], sem.at[c]))
        copies[-1].start()
    for copy in copies:
        copy.wait()


def correlate(me, place, blocks):
    inner, local, spectra = blocks[0].shape
    total = len(blocks) * local
    shape = (inner // 2, 2, local, total)
    vmem = pl.BlockSpec(memory_space=pltpu.VMEM)
    return pl.pallas_call(
        correlate_kernel,
        out_shape=jax.ShapeDtypeStruct(shape, F32),
        in_specs=[pl.BlockSpec(memory_space=pltpu.SMEM), vmem] + [vmem] * len(blocks),
        out_specs=pl.BlockSpec(memory_space=pltpu.HBM),
        scratch_shapes=[
            pltpu.VMEM((inner // 2, total, 2 * spectra), BF16),
            pltpu.VMEM(shape, F32),
            pltpu.SemaphoreType.DMA((inner // 2,)),
        ],
        compiler_params=pltpu.CompilerParams(vmem_limit_bytes=48 << 20),
        name="correlate",
    )(me, place, *blocks)


def body(groups, owners, voltages, weights, antenna_slot_index, station_order):
    group, tile = lax.axis_index("sgroup").astype(jnp.int32), lax.axis_index("tile").astype(jnp.int32)
    far = groups // 2

    def exchange(value, axis, size, bit):
        return lax.ppermute(value, axis, [(i, i ^ bit) for i in range(size)])

    def share(value, bit):
        return exchange(value, "sgroup", groups, bit)

    keep, send = beam(owners, tile[None], antenna_slot_index, jnp.transpose(weights, (0, 1, 3, 4, 2)), voltages)
    total = keep + exchange(send, "tile", owners, 1).astype(F32)
    bit = 2
    while bit < owners:
        sent = exchange(total[1::2].astype(BF16), "tile", owners, bit)
        total = total[0::2] + sent.astype(F32)
        bit *= 2
    own = total[0].astype(BF16)
    blocks = {0: own, far: share(own, far)}
    for i in range(far - 2, 0, -1):
        blocks[i] = share(own, i)
    both = share(jnp.stack([own, blocks[far]]), far - 1)
    blocks[far - 1], blocks[far + far - 1] = both[0], both[1]
    for i in range(1, far - 1):
        blocks[far + i] = share(blocks[far], i)
    place = placement(group[None], station_order, voltages.shape[3], own.shape[1])
    return correlate(group[None], place, [blocks[i] for i in range(groups)])


def solution(mesh):
    groups = mesh.shape["sgroup"]
    in_specs = (
        P(None, "sgroup", "tile", None, None, None),
        P(None, "sgroup", None, None, None),
        P("sgroup", "tile"),
        P(),
    )
    run = functools.partial(body, groups, mesh.shape["tile"])
    return jax.shard_map(run, mesh=mesh, in_specs=in_specs, out_specs=P("tile", None, "sgroup", None), check_vma=False)
```

```python
import functools

import jax
import jax.numpy as jnp
from jax import lax
from jax.experimental import pallas as pl
from jax.experimental.pallas import tpu as pltpu
from jax.sharding import PartitionSpec as P


F32, BF16 = jnp.float32, jnp.bfloat16


def iota(shape, axis):
    return lax.broadcasted_iota(jnp.int32, shape, axis)


def dot(left, right):
    return jnp.dot(left, right, preferred_element_type=F32)


def beam_kernel(owners, me_ref, index_hbm, w_hbm, v_hbm, keep_ref, send_ref, index_ref, w_ref, v_ref, left_ref, acc_ref, small_sem, v_sem):
    _, stations, antennas, polars, channels, spectra = v_ref.shape
    numbers = w_ref.shape[-1]
    per_owner = channels // owners
    rows = 2 * channels
    me = me_ref[0]
    copies = [pltpu.make_async_copy(index_hbm, index_ref, small_sem.at[0]), pltpu.make_async_copy(w_hbm, w_ref, small_sem.at[1])]
    spans = [(s, min(s + 2, stations)) for s in range(0, stations - 2, 2)] + [(s, s + 1) for s in range(max(stations - 2, 0), stations)]
    arrivals = {a: pltpu.make_async_copy(v_hbm.at[:, a:b], v_ref.at[:, a:b], v_sem.at[a]) for a, b in spans}
    for copy in copies:
        copy.start(priority=0)
    for copy in arrivals.values():
        copy.start(priority=1)

    spread = jnp.where(iota((antennas, antennas * channels), 1) // channels == iota((antennas, antennas * channels), 0), 1.0, 0.0).astype(BF16)
    lane_tile = min(128, antennas * channels)
    mask = iota((rows, lane_tile), 1) % channels == iota((rows, lane_tile), 0) % channels
    number = iota((numbers, antennas), 0)
    for copy in copies:
        copy.wait()
    compact = []
    for s in range(stations):
        chosen = jnp.where(number == index_ref[s : s + 1, :], 1.0, 0.0).astype(BF16)
        lines = jnp.concatenate([w_ref[k, s, p] for p in range(polars) for k in range(2)], axis=0)
        compact.append(dot(lines, chosen).astype(BF16))
    for s in range(stations):
        wide = dot(compact[s], spread)
        for p in range(polars):
            for i in range(0, antennas * channels, lane_tile):
                part = wide[p * rows : (p + 1) * rows, i : i + lane_tile]
                left_ref[s, p, :, i : i + lane_tile] = jnp.where(mask, part, 0.0).astype(BF16)

    def order_rows(stop, size):
        for slot in range(owners):
            target = send_ref if slot % 2 else keep_ref
            first = (stop - size) * polars * rows + (me ^ slot) * per_owner
            for part in range(2):
                for c in range(per_owner):
                    line = acc_ref[pl.ds(first + part * channels + c, size * polars, stride=rows), :]
                    target[slot // 2, part * per_owner + c, (stop - size) * polars : stop * polars] = line.astype(target.dtype)

    batch = 4 if stations % 4 == 0 else stations
    for s in range(stations):
        if s in arrivals:
            arrivals[s].wait()
        for p in range(polars):
            left = left_ref[s, p]
            real = dot(left, v_ref[0, s, :, p].reshape(antennas * channels, spectra))
            imag = dot(left, v_ref[1, s, :, p].reshape(antennas * channels, spectra))
            at = (s * polars + p) * rows
            acc_ref[at : at + channels, :] = real[:channels] - imag[channels:]
            acc_ref[at + channels : at + rows, :] = real[channels:] + imag[:channels]
        if (s + 1) % batch == 0:
            order_rows(s + 1, batch)


def beam(owners, me, index, weights, voltages):
    _, stations, antennas, polars, channels, spectra = voltages.shape
    rows = 2 * channels
    half = (owners // 2, rows // owners, stations * polars, spectra)
    hbm, vmem = pl.BlockSpec(memory_space=pltpu.HBM), pl.BlockSpec(memory_space=pltpu.VMEM)
    return pl.pallas_call(
        functools.partial(beam_kernel, owners),
        out_shape=(jax.ShapeDtypeStruct(half, F32), jax.ShapeDtypeStruct(half, BF16)),
        in_specs=[pl.BlockSpec(memory_space=pltpu.SMEM), hbm, hbm, hbm],
        out_specs=[vmem, vmem],
        scratch_shapes=[
            pltpu.VMEM(index.shape, jnp.int32),
            pltpu.VMEM(weights.shape, BF16),
            pltpu.VMEM(voltages.shape, BF16),
            pltpu.VMEM((stations, polars, rows, antennas * channels), BF16),
            pltpu.VMEM((stations * polars * rows, spectra), F32),
            pltpu.SemaphoreType.DMA((2,)),
            pltpu.SemaphoreType.DMA((stations,)),
        ],
        compiler_params=pltpu.CompilerParams(vmem_limit_bytes=48 << 20),
        name="beam",
    )(me, *(pltpu.with_memory_space_constraint(a, pltpu.HBM) for a in (index, weights, voltages)))


def place_kernel(local, polars, me_ref, order_ref, place_ref):
    total, stations = place_ref.shape[0], order_ref.shape[1]
    owns = jnp.where(order_ref[...] == iota((total, stations), 0) // polars, 1.0, 0.0).astype(BF16)
    column = iota((stations, total), 1)
    slot = ((column // local) ^ me_ref[0]) * (local // polars) + (column % local) // polars
    slots = jnp.where(iota((stations, total), 0) == slot, 1.0, 0.0).astype(BF16)
    same = iota((total, total), 0) % polars == iota((total, total), 1) % polars
    place_ref[...] = jnp.where(same, dot(owns, slots), 0.0).astype(BF16)


def placement(me, order, polars, local):
    vmem = pl.BlockSpec(memory_space=pltpu.VMEM)
    total = order.shape[0] * polars
    return pl.pallas_call(
        functools.partial(place_kernel, local, polars),
        out_shape=jax.ShapeDtypeStruct((total, total), BF16),
        in_specs=[pl.BlockSpec(memory_space=pltpu.SMEM), vmem],
        out_specs=vmem,
        compiler_params=pltpu.CompilerParams(vmem_limit_bytes=48 << 20),
        name="place",
    )(me, order[None, :])


def correlate_kernel(me_ref, place_ref, *refs):
    blocks, (out_hbm, row_ref, out_ref, sem) = refs[:-4], refs[-4:]
    inner, local, spectra = blocks[0].shape
    channels = inner // 2
    me, place = me_ref[0], place_ref[...]
    scale = 1.0 / spectra
    for c in range(channels):
        real = jnp.concatenate([b[c] for b in blocks], axis=0)
        imag = jnp.concatenate([b[channels + c] for b in blocks], axis=0)
        row_ref[c] = dot(place, jnp.concatenate([real, imag], axis=1)).astype(BF16)
    rows, copies = pl.ds(pl.multiple_of(me * local, local), local), []
    for c in range(channels):
        mine = row_ref[c, rows, :]
        left = jnp.concatenate(
            [mine, jnp.concatenate([mine[:, spectra:], -mine[:, :spectra]], axis=1)], axis=0
        )
        vis = lax.dot_general(left, row_ref[c], (((1,), (1,)), ((), ())), preferred_element_type=F32) * scale
        out_ref[c, 0] = vis[:local]
        out_ref[c, 1] = vis[local:]
        copies.append(pltpu.make_async_copy(out_ref.at[c], out_hbm.at[c], sem.at[c]))
        copies[-1].start()
    for copy in copies:
        copy.wait()


def correlate(me, place, blocks):
    inner, local, spectra = blocks[0].shape
    total = len(blocks) * local
    shape = (inner // 2, 2, local, total)
    vmem = pl.BlockSpec(memory_space=pltpu.VMEM)
    return pl.pallas_call(
        correlate_kernel,
        out_shape=jax.ShapeDtypeStruct(shape, F32),
        in_specs=[pl.BlockSpec(memory_space=pltpu.SMEM), vmem] + [vmem] * len(blocks),
        out_specs=pl.BlockSpec(memory_space=pltpu.HBM),
        scratch_shapes=[
            pltpu.VMEM((inner // 2, total, 2 * spectra), BF16),
            pltpu.VMEM(shape, F32),
            pltpu.SemaphoreType.DMA((inner // 2,)),
        ],
        compiler_params=pltpu.CompilerParams(vmem_limit_bytes=48 << 20),
        name="correlate",
    )(me, place, *blocks)


def body(groups, owners, voltages, weights, antenna_slot_index, station_order):
    group, tile = lax.axis_index("sgroup").astype(jnp.int32), lax.axis_index("tile").astype(jnp.int32)
    far = groups // 2

    def exchange(value, axis, size, bit):
        return lax.ppermute(value, axis, [(i, i ^ bit) for i in range(size)])

    def share(value, bit):
        return exchange(value, "sgroup", groups, bit)

    keep, send = beam(owners, tile[None], antenna_slot_index, jnp.transpose(weights, (0, 1, 3, 4, 2)), voltages)
    total = keep + exchange(send, "tile", owners, 1).astype(F32)
    bit = 2
    while bit < owners:
        sent = total[1::2].astype(F32 if 2 * bit < owners else BF16)
        sent = exchange(sent, "tile", owners, bit)
        total = total[0::2] + sent.astype(F32)
        bit *= 2
    own = total[0].astype(BF16)
    blocks = {0: own, far: share(own, far)}
    for i in range(far - 2, 0, -1):
        blocks[i] = share(own, i)
    both = share(jnp.stack([own, blocks[far]]), far - 1)
    blocks[far - 1], blocks[far + far - 1] = both[0], both[1]
    for i in range(1, far - 1):
        blocks[far + i] = share(blocks[far], i)
    place = placement(group[None], station_order, voltages.shape[3], own.shape[1])
    return correlate(group[None], place, [blocks[i] for i in range(groups)])


def solution(mesh):
    groups, owners = mesh.shape["sgroup"], mesh.shape["tile"]
    in_specs = (
        P(None, "sgroup", "tile", None, None, None),
        P(None, "sgroup", None, None, None),
        P("sgroup", "tile"),
        P(),
    )
    run = functools.partial(body, groups, owners)
    return jax.shard_map(run, mesh=mesh, in_specs=in_specs, out_specs=P("tile", None, "sgroup", None), check_vma=False)
```

```python
import functools

import jax
import jax.numpy as jnp
from jax import lax
from jax.experimental import pallas as pl
from jax.experimental.pallas import tpu as pltpu
from jax.sharding import PartitionSpec as P


F32, BF16 = jnp.float32, jnp.bfloat16


def iota(shape, axis):
    return lax.broadcasted_iota(jnp.int32, shape, axis)


def dot(left, right):
    return jnp.dot(left, right, preferred_element_type=F32)


def beam_kernel(owners, me_ref, index_hbm, w_hbm, v_hbm, keep_ref, send_ref, index_ref, w_ref, v_ref, left_ref, acc_ref, small_sem, v_sem):
    _, stations, antennas, polars, channels, spectra = v_ref.shape
    numbers = w_ref.shape[-1]
    per_owner = channels // owners
    rows = 2 * channels
    me = me_ref[0]
    copies = [pltpu.make_async_copy(index_hbm, index_ref, small_sem.at[0]), pltpu.make_async_copy(w_hbm, w_ref, small_sem.at[1])]
    spans = [(s, min(s + 2, stations)) for s in range(0, stations - 2, 2)] + [(s, s + 1) for s in range(max(stations - 2, 0), stations)]
    arrivals = {a: pltpu.make_async_copy(v_hbm.at[:, a:b], v_ref.at[:, a:b], v_sem.at[a]) for a, b in spans}
    for copy in copies:
        copy.start(priority=0)
    for copy in arrivals.values():
        copy.start(priority=1)

    spread = jnp.where(iota((antennas, antennas * channels), 1) // channels == iota((antennas, antennas * channels), 0), 1.0, 0.0).astype(BF16)
    lane_tile = min(128, antennas * channels)
    mask = iota((rows, lane_tile), 1) % channels == iota((rows, lane_tile), 0) % channels
    number = iota((numbers, antennas), 0)
    for copy in copies:
        copy.wait()
    compact = []
    for s in range(stations):
        chosen = jnp.where(number == index_ref[s : s + 1, :], 1.0, 0.0).astype(BF16)
        lines = jnp.concatenate([w_ref[k, s, p] for p in range(polars) for k in range(2)], axis=0)
        compact.append(dot(lines, chosen).astype(BF16))
    for s in range(stations):
        wide = dot(compact[s], spread)
        for p in range(polars):
            for i in range(0, antennas * channels, lane_tile):
                part = wide[p * rows : (p + 1) * rows, i : i + lane_tile]
                left_ref[s, p, :, i : i + lane_tile] = jnp.where(mask, part, 0.0).astype(BF16)

    def order_rows(stop, size):
        for slot in range(owners):
            target = send_ref if slot % 2 else keep_ref
            first = (stop - size) * polars * rows + (me ^ slot) * per_owner
            for part in range(2):
                for c in range(per_owner):
                    line = acc_ref[pl.ds(first + part * channels + c, size * polars, stride=rows), :]
                    target[slot // 2, part * per_owner + c, (stop - size) * polars : stop * polars] = line.astype(target.dtype)

    batch = 4 if stations % 4 == 0 else stations
    for s in range(stations):
        if s in arrivals:
            arrivals[s].wait()
        for p in range(polars):
            left = left_ref[s, p]
            real = dot(left, v_ref[0, s, :, p].reshape(antennas * channels, spectra))
            imag = dot(left, v_ref[1, s, :, p].reshape(antennas * channels, spectra))
            at = (s * polars + p) * rows
            acc_ref[at : at + channels, :] = real[:channels] - imag[channels:]
            acc_ref[at + channels : at + rows, :] = real[channels:] + imag[:channels]
        if (s + 1) % batch == 0:
            order_rows(s + 1, batch)


def beam(owners, me, index, weights, voltages):
    _, stations, antennas, polars, channels, spectra = voltages.shape
    rows = 2 * channels
    half = (owners // 2, rows // owners, stations * polars, spectra)
    hbm, vmem = pl.BlockSpec(memory_space=pltpu.HBM), pl.BlockSpec(memory_space=pltpu.VMEM)
    return pl.pallas_call(
        functools.partial(beam_kernel, owners),
        out_shape=(jax.ShapeDtypeStruct(half, F32), jax.ShapeDtypeStruct(half, BF16)),
        in_specs=[pl.BlockSpec(memory_space=pltpu.SMEM), hbm, hbm, hbm],
        out_specs=[vmem, vmem],
        scratch_shapes=[
            pltpu.VMEM(index.shape, jnp.int32),
            pltpu.VMEM(weights.shape, BF16),
            pltpu.VMEM(voltages.shape, BF16),
            pltpu.VMEM((stations, polars, rows, antennas * channels), BF16),
            pltpu.VMEM((stations * polars * rows, spectra), F32),
            pltpu.SemaphoreType.DMA((2,)),
            pltpu.SemaphoreType.DMA((stations,)),
        ],
        compiler_params=pltpu.CompilerParams(vmem_limit_bytes=48 << 20),
        name="beam",
    )(me, *(pltpu.with_memory_space_constraint(a, pltpu.HBM) for a in (index, weights, voltages)))


def place_kernel(local, polars, me_ref, order_ref, place_ref):
    total, stations = place_ref.shape[0], order_ref.shape[1]
    owns = jnp.where(order_ref[...] == iota((total, stations), 0) // polars, 1.0, 0.0).astype(BF16)
    column = iota((stations, total), 1)
    block, far = column // local, total // local // 2
    block = jnp.where(block == far, far - 1, jnp.where(block == far - 1, far, block))
    slot = (block ^ me_ref[0]) * (local // polars) + (column % local) // polars
    slots = jnp.where(iota((stations, total), 0) == slot, 1.0, 0.0).astype(BF16)
    same = iota((total, total), 0) % polars == iota((total, total), 1) % polars
    place_ref[...] = jnp.where(same, dot(owns, slots), 0.0).astype(BF16)


def placement(me, order, polars, local):
    vmem = pl.BlockSpec(memory_space=pltpu.VMEM)
    total = order.shape[0] * polars
    return pl.pallas_call(
        functools.partial(place_kernel, local, polars),
        out_shape=jax.ShapeDtypeStruct((total, total), BF16),
        in_specs=[pl.BlockSpec(memory_space=pltpu.SMEM), vmem],
        out_specs=vmem,
        compiler_params=pltpu.CompilerParams(vmem_limit_bytes=48 << 20),
        name="place",
    )(me, order[None, :])


def both_parts(blocks, c, channels):
    real = jnp.concatenate([b[c] for b in blocks], axis=0)
    imag = jnp.concatenate([b[channels + c] for b in blocks], axis=0)
    return jnp.concatenate([real, imag], axis=1)


def early_kernel(place_ref, *refs):
    blocks, row_ref = refs[:-1], refs[-1]
    place = place_ref[:, : place_ref.shape[1] // 2]
    channels = row_ref.shape[0]
    for c in range(channels):
        row_ref[c] = dot(place, both_parts(blocks, c, channels)).astype(BF16)


def early(place, blocks):
    inner, _, spectra = blocks[0].shape
    vmem = pl.BlockSpec(memory_space=pltpu.VMEM)
    return pl.pallas_call(
        early_kernel,
        out_shape=jax.ShapeDtypeStruct((inner // 2, place.shape[0], 2 * spectra), BF16),
        in_specs=[vmem] * (1 + len(blocks)),
        out_specs=vmem,
        compiler_params=pltpu.CompilerParams(vmem_limit_bytes=48 << 20),
        name="early",
    )(place, *blocks)


def correlate_kernel(me_ref, place_ref, early_ref, *refs):
    blocks, (out_hbm, row_ref, out_ref, sem) = refs[:-4], refs[-4:]
    inner, local, spectra = blocks[0].shape
    channels = inner // 2
    me, place = me_ref[0], place_ref[:, place_ref.shape[1] // 2 :]
    scale = 1.0 / spectra
    for c in range(channels):
        row_ref[c] = dot(place, both_parts(blocks, c, channels)).astype(BF16) + early_ref[c]
    rows, copies = pl.ds(pl.multiple_of(me * local, local), local), []
    for c in range(channels):
        mine = row_ref[c, rows, :]
        left = jnp.concatenate(
            [mine, jnp.concatenate([mine[:, spectra:], -mine[:, :spectra]], axis=1)], axis=0
        )
        vis = lax.dot_general(left, row_ref[c], (((1,), (1,)), ((), ())), preferred_element_type=F32) * scale
        out_ref[c, 0] = vis[:local]
        out_ref[c, 1] = vis[local:]
        copies.append(pltpu.make_async_copy(out_ref.at[c], out_hbm.at[c], sem.at[c]))
        copies[-1].start()
    for copy in copies:
        copy.wait()


def correlate(me, place, ordered, blocks):
    inner, local, spectra = blocks[0].shape
    total = place.shape[0]
    shape = (inner // 2, 2, local, total)
    vmem = pl.BlockSpec(memory_space=pltpu.VMEM)
    return pl.pallas_call(
        correlate_kernel,
        out_shape=jax.ShapeDtypeStruct(shape, F32),
        in_specs=[pl.BlockSpec(memory_space=pltpu.SMEM)] + [vmem] * (2 + len(blocks)),
        out_specs=pl.BlockSpec(memory_space=pltpu.HBM),
        scratch_shapes=[
            pltpu.VMEM((inner // 2, total, 2 * spectra), BF16),
            pltpu.VMEM(shape, F32),
            pltpu.SemaphoreType.DMA((inner // 2,)),
        ],
        compiler_params=pltpu.CompilerParams(vmem_limit_bytes=48 << 20),
        name="correlate",
    )(me, place, ordered, *blocks)


def body(groups, owners, voltages, weights, antenna_slot_index, station_order):
    group, tile = lax.axis_index("sgroup").astype(jnp.int32), lax.axis_index("tile").astype(jnp.int32)
    far = groups // 2

    def exchange(value, axis, size, bit):
        return lax.ppermute(value, axis, [(i, i ^ bit) for i in range(size)])

    def share(value, bit):
        return exchange(value, "sgroup", groups, bit)

    keep, send = beam(owners, tile[None], antenna_slot_index, jnp.transpose(weights, (0, 1, 3, 4, 2)), voltages)
    total = keep + exchange(send, "tile", owners, 1).astype(F32)
    bit = 2
    while bit < owners:
        sent = total[1::2].astype(F32 if 2 * bit < owners else BF16)
        sent = exchange(sent, "tile", owners, bit)
        total = total[0::2] + sent.astype(F32)
        bit *= 2
    own = total[0].astype(BF16)
    blocks = {0: own, far: share(own, far)}
    for i in range(far - 2, 0, -1):
        blocks[i] = share(own, i)
    both = share(jnp.stack([own, blocks[far]]), far - 1)
    blocks[far - 1], blocks[far + far - 1] = both[0], both[1]
    for i in range(1, far - 1):
        blocks[far + i] = share(blocks[far], i)
    place = placement(group[None], station_order, voltages.shape[3], own.shape[1])
    first = [*range(far - 1), far]
    ordered = early(place, [blocks[i] for i in first])
    return correlate(group[None], place, ordered, [blocks[i] for i in range(groups) if i not in first])


def solution(mesh):
    groups, owners = mesh.shape["sgroup"], mesh.shape["tile"]
    in_specs = (
        P(None, "sgroup", "tile", None, None, None),
        P(None, "sgroup", None, None, None),
        P("sgroup", "tile"),
        P(),
    )
    run = functools.partial(body, groups, owners)
    return jax.shard_map(run, mesh=mesh, in_specs=in_specs, out_specs=P("tile", None, "sgroup", None), check_vma=False)
```

```python
import functools

import jax
import jax.numpy as jnp
from jax import lax
from jax.experimental import pallas as pl
from jax.experimental.pallas import tpu as pltpu
from jax.sharding import PartitionSpec as P


F32, BF16 = jnp.float32, jnp.bfloat16


def iota(shape, axis):
    return lax.broadcasted_iota(jnp.int32, shape, axis)


def dot(left, right):
    return jnp.dot(left, right, preferred_element_type=F32)


def beam_kernel(owners, me_ref, index_hbm, w_hbm, v_hbm, keep_ref, send_ref, index_ref, w_ref, v_ref, left_ref, acc_ref, small_sem, v_sem):
    _, stations, antennas, polars, channels, spectra = v_ref.shape
    numbers = w_ref.shape[-1]
    per_owner = channels // owners
    rows = 2 * channels
    me = me_ref[0]
    copies = [pltpu.make_async_copy(index_hbm, index_ref, small_sem.at[0]), pltpu.make_async_copy(w_hbm, w_ref, small_sem.at[1])]
    spans = [(s, min(s + 2, stations)) for s in range(0, stations - 2, 2)] + [(s, s + 1) for s in range(max(stations - 2, 0), stations)]
    arrivals = {a: pltpu.make_async_copy(v_hbm.at[:, a:b], v_ref.at[:, a:b], v_sem.at[a]) for a, b in spans}
    for copy in copies:
        copy.start(priority=0)
    for copy in arrivals.values():
        copy.start(priority=1)

    spread = jnp.where(iota((antennas, antennas * channels), 1) // channels == iota((antennas, antennas * channels), 0), 1.0, 0.0).astype(BF16)
    lane_tile = min(128, antennas * channels)
    mask = iota((rows, lane_tile), 1) % channels == iota((rows, lane_tile), 0) % channels
    number = iota((numbers, antennas), 0)
    for copy in copies:
        copy.wait()
    compact = []
    for s in range(stations):
        chosen = jnp.where(number == index_ref[s : s + 1, :], 1.0, 0.0).astype(BF16)
        lines = jnp.concatenate([w_ref[k, s, p] for p in range(polars) for k in range(2)], axis=0)
        compact.append(dot(lines, chosen).astype(BF16))
    for s in range(stations):
        wide = dot(compact[s], spread)
        for p in range(polars):
            for i in range(0, antennas * channels, lane_tile):
                part = wide[p * rows : (p + 1) * rows, i : i + lane_tile]
                left_ref[s, p, :, i : i + lane_tile] = jnp.where(mask, part, 0.0).astype(BF16)

    def order_rows(stop, size):
        for slot in range(owners):
            target = send_ref if slot % 2 else keep_ref
            first = (stop - size) * polars * rows + (me ^ slot) * per_owner
            for part in range(2):
                for c in range(per_owner):
                    line = acc_ref[pl.ds(first + part * channels + c, size * polars, stride=rows), :]
                    target[slot // 2, part * per_owner + c, (stop - size) * polars : stop * polars] = line.astype(target.dtype)

    batch = 4 if stations % 4 == 0 else stations
    for s in range(stations):
        if s in arrivals:
            arrivals[s].wait()
        for p in range(polars):
            left = left_ref[s, p]
            real = dot(left, v_ref[0, s, :, p].reshape(antennas * channels, spectra))
            imag = dot(left, v_ref[1, s, :, p].reshape(antennas * channels, spectra))
            at = (s * polars + p) * rows
            acc_ref[at : at + channels, :] = real[:channels] - imag[channels:]
            acc_ref[at + channels : at + rows, :] = real[channels:] + imag[:channels]
        if (s + 1) % batch == 0:
            order_rows(s + 1, batch)


def beam(owners, me, index, weights, voltages):
    _, stations, antennas, polars, channels, spectra = voltages.shape
    rows = 2 * channels
    half = (owners // 2, rows // owners, stations * polars, spectra)
    hbm, vmem = pl.BlockSpec(memory_space=pltpu.HBM), pl.BlockSpec(memory_space=pltpu.VMEM)
    return pl.pallas_call(
        functools.partial(beam_kernel, owners),
        out_shape=(jax.ShapeDtypeStruct(half, F32), jax.ShapeDtypeStruct(half, BF16)),
        in_specs=[pl.BlockSpec(memory_space=pltpu.SMEM), hbm, hbm, hbm],
        out_specs=[vmem, vmem],
        scratch_shapes=[
            pltpu.VMEM(index.shape, jnp.int32),
            pltpu.VMEM(weights.shape, BF16),
            pltpu.VMEM(voltages.shape, BF16),
            pltpu.VMEM((stations, polars, rows, antennas * channels), BF16),
            pltpu.VMEM((stations * polars * rows, spectra), F32),
            pltpu.SemaphoreType.DMA((2,)),
            pltpu.SemaphoreType.DMA((stations,)),
        ],
        compiler_params=pltpu.CompilerParams(vmem_limit_bytes=48 << 20),
        name="beam",
    )(me, *(pltpu.with_memory_space_constraint(a, pltpu.HBM) for a in (index, weights, voltages)))


def place_kernel(local, polars, me_ref, order_ref, place_ref):
    total, stations = place_ref.shape[0], order_ref.shape[1]
    owns = jnp.where(order_ref[...] == iota((total, stations), 0) // polars, 1.0, 0.0).astype(BF16)
    column = iota((stations, total), 1)
    block, far = column // local, total // local // 2
    block = jnp.where(block == far, far - 1, jnp.where(block == far - 1, far, block))
    slot = (block ^ me_ref[0]) * (local // polars) + (column % local) // polars
    slots = jnp.where(iota((stations, total), 0) == slot, 1.0, 0.0).astype(BF16)
    same = iota((total, total), 0) % polars == iota((total, total), 1) % polars
    place_ref[...] = jnp.where(same, dot(owns, slots), 0.0).astype(BF16)


def placement(me, order, polars, local):
    vmem = pl.BlockSpec(memory_space=pltpu.VMEM)
    total = order.shape[0] * polars
    return pl.pallas_call(
        functools.partial(place_kernel, local, polars),
        out_shape=jax.ShapeDtypeStruct((total, total), BF16),
        in_specs=[pl.BlockSpec(memory_space=pltpu.SMEM), vmem],
        out_specs=vmem,
        compiler_params=pltpu.CompilerParams(vmem_limit_bytes=48 << 20),
        name="place",
    )(me, order[None, :])


def both_parts(blocks, c, channels):
    real = jnp.concatenate([b[c] for b in blocks], axis=0)
    imag = jnp.concatenate([b[channels + c] for b in blocks], axis=0)
    return jnp.concatenate([real, imag], axis=1)


def early_kernel(place_ref, *refs):
    blocks, row_ref = refs[:-1], refs[-1]
    place = place_ref[:, : place_ref.shape[1] // 2]
    channels = row_ref.shape[0]
    for c in range(channels):
        row_ref[c] = dot(place, both_parts(blocks, c, channels)).astype(BF16)


def early(place, blocks):
    inner, _, spectra = blocks[0].shape
    vmem = pl.BlockSpec(memory_space=pltpu.VMEM)
    return pl.pallas_call(
        early_kernel,
        out_shape=jax.ShapeDtypeStruct((inner // 2, place.shape[0], 2 * spectra), BF16),
        in_specs=[vmem] * (1 + len(blocks)),
        out_specs=vmem,
        compiler_params=pltpu.CompilerParams(vmem_limit_bytes=48 << 20),
        name="early",
    )(place, *blocks)


def correlate_kernel(me_ref, place_ref, early_ref, *refs):
    blocks, (out_hbm, row_ref, out_ref, sem) = refs[:-4], refs[-4:]
    inner, local, spectra = blocks[0].shape
    channels = inner // 2
    me, place = me_ref[0], place_ref[:, place_ref.shape[1] // 2 :]
    scale = 1.0 / spectra
    for c in range(channels):
        row_ref[c] = dot(place, both_parts(blocks, c, channels)).astype(BF16) + early_ref[c]
    rows, copies = pl.ds(pl.multiple_of(me * local, local), local), []
    for c in range(channels):
        mine = row_ref[c, rows, :]
        left = jnp.concatenate(
            [mine, jnp.concatenate([mine[:, spectra:], -mine[:, :spectra]], axis=1)], axis=0
        )
        vis = lax.dot_general(left, row_ref[c], (((1,), (1,)), ((), ())), preferred_element_type=F32) * scale
        out_ref[c, 0] = vis[:local]
        out_ref[c, 1] = vis[local:]
        copies.append(pltpu.make_async_copy(out_ref.at[c], out_hbm.at[c], sem.at[c]))
        copies[-1].start()
    for copy in copies:
        copy.wait()


def correlate(me, place, ordered, blocks):
    inner, local, spectra = blocks[0].shape
    total = place.shape[0]
    shape = (inner // 2, 2, local, total)
    vmem = pl.BlockSpec(memory_space=pltpu.VMEM)
    return pl.pallas_call(
        correlate_kernel,
        out_shape=jax.ShapeDtypeStruct(shape, F32),
        in_specs=[pl.BlockSpec(memory_space=pltpu.SMEM)] + [vmem] * (2 + len(blocks)),
        out_specs=pl.BlockSpec(memory_space=pltpu.HBM),
        scratch_shapes=[
            pltpu.VMEM((inner // 2, total, 2 * spectra), BF16),
            pltpu.VMEM(shape, F32),
            pltpu.SemaphoreType.DMA((inner // 2,)),
        ],
        compiler_params=pltpu.CompilerParams(vmem_limit_bytes=48 << 20),
        name="correlate",
    )(me, place, ordered, *blocks)


def body(groups, owners, voltages, weights, antenna_slot_index, station_order):
    group, tile = lax.axis_index("sgroup").astype(jnp.int32), lax.axis_index("tile").astype(jnp.int32)
    far = groups // 2

    def exchange(value, axis, size, bit):
        return lax.ppermute(value, axis, [(i, i ^ bit) for i in range(size)])

    def share(value, bit):
        return exchange(value, "sgroup", groups, bit)

    keep, send = beam(owners, tile[None], antenna_slot_index, jnp.transpose(weights, (0, 1, 3, 4, 2)), voltages)
    halves = [keep, exchange(send, "tile", owners, 1)]
    bit = 2
    while bit < owners:
        sent = sum(h[1::2].astype(F32) for h in halves).astype(F32 if 2 * bit < owners else BF16)
        sent = exchange(sent, "tile", owners, bit)
        halves = [h[0::2] for h in halves] + [sent]
        bit *= 2
    total = sum(h.astype(F32) for h in halves)
    own = total[0].astype(BF16)
    blocks = {0: own, far: share(own, far)}
    for i in range(far - 2, 0, -1):
        blocks[i] = share(own, i)
    both = share(jnp.stack([own, blocks[far]]), far - 1)
    blocks[far - 1], blocks[far + far - 1] = both[0], both[1]
    for i in range(1, far - 1):
        blocks[far + i] = share(blocks[far], i)
    place = placement(group[None], station_order, voltages.shape[3], own.shape[1])
    first = [*range(far - 1), far]
    ordered = early(place, [blocks[i] for i in first])
    return correlate(group[None], place, ordered, [blocks[i] for i in range(groups) if i not in first])


def solution(mesh):
    groups, owners = mesh.shape["sgroup"], mesh.shape["tile"]
    in_specs = (
        P(None, "sgroup", "tile", None, None, None),
        P(None, "sgroup", None, None, None),
        P("sgroup", "tile"),
        P(),
    )
    run = functools.partial(body, groups, owners)
    return jax.shard_map(run, mesh=mesh, in_specs=in_specs, out_specs=P("tile", None, "sgroup", None), check_vma=False)
```

```python
import functools

import jax
import jax.numpy as jnp
from jax import lax
from jax.experimental import pallas as pl
from jax.experimental.pallas import tpu as pltpu
from jax.sharding import PartitionSpec as P


F32, BF16 = jnp.float32, jnp.bfloat16


def iota(shape, axis):
    return lax.broadcasted_iota(jnp.int32, shape, axis)


def dot(left, right):
    return jnp.dot(left, right, preferred_element_type=F32)


def beam_kernel(owners, me_ref, index_hbm, w_hbm, v_hbm, keep_ref, send_ref, index_ref, w_ref, v_ref, left_ref, acc_ref, small_sem, v_sem):
    _, stations, antennas, polars, channels, spectra = v_ref.shape
    numbers = w_ref.shape[-1]
    per_owner = channels // owners
    rows = 2 * channels
    me = me_ref[0]
    copies = [pltpu.make_async_copy(index_hbm, index_ref, small_sem.at[0]), pltpu.make_async_copy(w_hbm, w_ref, small_sem.at[1])]
    spans = [(s, min(s + 2, stations)) for s in range(0, stations - 2, 2)] + [(s, s + 1) for s in range(max(stations - 2, 0), stations)]
    arrivals = {a: pltpu.make_async_copy(v_hbm.at[:, a:b], v_ref.at[:, a:b], v_sem.at[a]) for a, b in spans}
    for copy in copies:
        copy.start(priority=0)
    for copy in arrivals.values():
        copy.start(priority=1)

    spread = jnp.where(iota((antennas, antennas * channels), 1) // channels == iota((antennas, antennas * channels), 0), 1.0, 0.0).astype(BF16)
    lane_tile = min(128, antennas * channels)
    mask = iota((rows, lane_tile), 1) % channels == iota((rows, lane_tile), 0) % channels
    number = iota((numbers, antennas), 0)
    for copy in copies:
        copy.wait()
    compact = []
    for s in range(stations):
        chosen = jnp.where(number == index_ref[s : s + 1, :], 1.0, 0.0).astype(BF16)
        lines = jnp.concatenate([w_ref[k, s, p] for p in range(polars) for k in range(2)], axis=0)
        compact.append(dot(lines, chosen).astype(BF16))
    for s in range(stations):
        wide = dot(compact[s], spread)
        for p in range(polars):
            for i in range(0, antennas * channels, lane_tile):
                part = wide[p * rows : (p + 1) * rows, i : i + lane_tile]
                left_ref[s, p, :, i : i + lane_tile] = jnp.where(mask, part, 0.0).astype(BF16)

    def order_rows(stop, size):
        for slot in range(owners):
            target = send_ref if slot % 2 else keep_ref
            first = (stop - size) * polars * rows + (me ^ slot) * per_owner
            for part in range(2):
                for c in range(per_owner):
                    line = acc_ref[pl.ds(first + part * channels + c, size * polars, stride=rows), :]
                    target[slot // 2, part * per_owner + c, (stop - size) * polars : stop * polars] = line.astype(target.dtype)

    batch = 4 if stations % 4 == 0 else stations
    for s in range(stations):
        if s in arrivals:
            arrivals[s].wait()
        for p in range(polars):
            left = left_ref[s, p]
            real = dot(left, v_ref[0, s, :, p].reshape(antennas * channels, spectra))
            imag = dot(left, v_ref[1, s, :, p].reshape(antennas * channels, spectra))
            at = (s * polars + p) * rows
            acc_ref[at : at + channels, :] = real[:channels] - imag[channels:]
            acc_ref[at + channels : at + rows, :] = real[channels:] + imag[:channels]
        if (s + 1) % batch == 0:
            order_rows(s + 1, batch)


def beam(owners, me, index, weights, voltages):
    _, stations, antennas, polars, channels, spectra = voltages.shape
    rows = 2 * channels
    half = (owners // 2, rows // owners, stations * polars, spectra)
    hbm, vmem = pl.BlockSpec(memory_space=pltpu.HBM), pl.BlockSpec(memory_space=pltpu.VMEM)
    return pl.pallas_call(
        functools.partial(beam_kernel, owners),
        out_shape=(jax.ShapeDtypeStruct(half, F32), jax.ShapeDtypeStruct(half, BF16)),
        in_specs=[pl.BlockSpec(memory_space=pltpu.SMEM), hbm, hbm, hbm],
        out_specs=[vmem, vmem],
        scratch_shapes=[
            pltpu.VMEM(index.shape, jnp.int32),
            pltpu.VMEM(weights.shape, BF16),
            pltpu.VMEM(voltages.shape, BF16),
            pltpu.VMEM((stations, polars, rows, antennas * channels), BF16),
            pltpu.VMEM((stations * polars * rows, spectra), F32),
            pltpu.SemaphoreType.DMA((2,)),
            pltpu.SemaphoreType.DMA((stations,)),
        ],
        compiler_params=pltpu.CompilerParams(vmem_limit_bytes=48 << 20),
        name="beam",
    )(me, *(pltpu.with_memory_space_constraint(a, pltpu.HBM) for a in (index, weights, voltages)))


def place_kernel(local, polars, me_ref, order_ref, place_ref):
    total, stations = place_ref.shape[0], order_ref.shape[1]
    owns = jnp.where(order_ref[...] == iota((total, stations), 0) // polars, 1.0, 0.0).astype(BF16)
    column = iota((stations, total), 1)
    block, far = column // local, total // local // 2
    block = jnp.where(block == far, far - 1, jnp.where(block == far - 1, far, block))
    slot = (block ^ me_ref[0]) * (local // polars) + (column % local) // polars
    slots = jnp.where(iota((stations, total), 0) == slot, 1.0, 0.0).astype(BF16)
    same = iota((total, total), 0) % polars == iota((total, total), 1) % polars
    place_ref[...] = jnp.where(same, dot(owns, slots), 0.0).astype(BF16)


def placement(me, order, polars, local):
    vmem = pl.BlockSpec(memory_space=pltpu.VMEM)
    total = order.shape[0] * polars
    return pl.pallas_call(
        functools.partial(place_kernel, local, polars),
        out_shape=jax.ShapeDtypeStruct((total, total), BF16),
        in_specs=[pl.BlockSpec(memory_space=pltpu.SMEM), vmem],
        out_specs=vmem,
        compiler_params=pltpu.CompilerParams(vmem_limit_bytes=48 << 20),
        name="place",
    )(me, order[None, :])


def both_parts(blocks, c, channels):
    real = jnp.concatenate([b[c] for b in blocks], axis=0)
    imag = jnp.concatenate([b[channels + c] for b in blocks], axis=0)
    return jnp.concatenate([real, imag], axis=1)


def early_kernel(place_ref, *refs):
    blocks, row_ref = refs[:-1], refs[-1]
    place = place_ref[:, : place_ref.shape[1] // 2]
    channels = row_ref.shape[0]
    for c in range(channels):
        row_ref[c] = dot(place, both_parts(blocks, c, channels)).astype(BF16)


def early(place, blocks):
    inner, _, spectra = blocks[0].shape
    vmem = pl.BlockSpec(memory_space=pltpu.VMEM)
    return pl.pallas_call(
        early_kernel,
        out_shape=jax.ShapeDtypeStruct((inner // 2, place.shape[0], 2 * spectra), BF16),
        in_specs=[vmem] * (1 + len(blocks)),
        out_specs=vmem,
        compiler_params=pltpu.CompilerParams(vmem_limit_bytes=48 << 20),
        name="early",
    )(place, *blocks)


def correlate_kernel(me_ref, place_ref, early_ref, *refs):
    blocks, (out_hbm, row_ref, out_ref, sem) = refs[:-4], refs[-4:]
    inner, local, spectra = blocks[0].shape
    channels = inner // 2
    me, place = me_ref[0], place_ref[:, place_ref.shape[1] // 2 :]
    scale = 1.0 / spectra
    rows, copies, mine_of = pl.ds(pl.multiple_of(me * local, local), local), [], []
    mine_place = place_ref[rows, place_ref.shape[1] // 2 :]
    for c in range(channels):
        late = both_parts(blocks, c, channels)
        row_ref[c] = dot(place, late).astype(BF16) + early_ref[c]
        mine_of.append(dot(mine_place, late).astype(BF16) + early_ref[c, rows, :])
    for c in range(channels):
        mine = mine_of[c]
        left = jnp.concatenate(
            [mine, jnp.concatenate([mine[:, spectra:], -mine[:, :spectra]], axis=1)], axis=0
        )
        vis = lax.dot_general(left, row_ref[c], (((1,), (1,)), ((), ())), preferred_element_type=F32) * scale
        out_ref[c, 0] = vis[:local]
        out_ref[c, 1] = vis[local:]
        copies.append(pltpu.make_async_copy(out_ref.at[c], out_hbm.at[c], sem.at[c]))
        copies[-1].start()
    for copy in copies:
        copy.wait()


def correlate(me, place, ordered, blocks):
    inner, local, spectra = blocks[0].shape
    total = place.shape[0]
    shape = (inner // 2, 2, local, total)
    vmem = pl.BlockSpec(memory_space=pltpu.VMEM)
    return pl.pallas_call(
        correlate_kernel,
        out_shape=jax.ShapeDtypeStruct(shape, F32),
        in_specs=[pl.BlockSpec(memory_space=pltpu.SMEM)] + [vmem] * (2 + len(blocks)),
        out_specs=pl.BlockSpec(memory_space=pltpu.HBM),
        scratch_shapes=[
            pltpu.VMEM((inner // 2, total, 2 * spectra), BF16),
            pltpu.VMEM(shape, F32),
            pltpu.SemaphoreType.DMA((inner // 2,)),
        ],
        compiler_params=pltpu.CompilerParams(vmem_limit_bytes=48 << 20),
        name="correlate",
    )(me, place, ordered, *blocks)


def body(groups, owners, voltages, weights, antenna_slot_index, station_order):
    group, tile = lax.axis_index("sgroup").astype(jnp.int32), lax.axis_index("tile").astype(jnp.int32)
    far = groups // 2

    def exchange(value, axis, size, bit):
        return lax.ppermute(value, axis, [(i, i ^ bit) for i in range(size)])

    def share(value, bit):
        return exchange(value, "sgroup", groups, bit)

    keep, send = beam(owners, tile[None], antenna_slot_index, jnp.transpose(weights, (0, 1, 3, 4, 2)), voltages)
    total = keep + exchange(send, "tile", owners, 1).astype(F32)
    bit = 2
    while bit < owners:
        sent = total[1::2].astype(F32 if 2 * bit < owners else BF16)
        sent = exchange(sent, "tile", owners, bit)
        total = total[0::2] + sent.astype(F32)
        bit *= 2
    own = total[0].astype(BF16)
    blocks = {0: own, far: share(own, far)}
    for i in range(far - 2, 0, -1):
        blocks[i] = share(own, i)
    both = share(jnp.stack([own, blocks[far]]), far - 1)
    blocks[far - 1], blocks[far + far - 1] = both[0], both[1]
    for i in range(1, far - 1):
        blocks[far + i] = share(blocks[far], i)
    place = placement(group[None], station_order, voltages.shape[3], own.shape[1])
    first = [*range(far - 1), far]
    ordered = early(place, [blocks[i] for i in first])
    return correlate(group[None], place, ordered, [blocks[i] for i in range(groups) if i not in first])


def solution(mesh):
    groups, owners = mesh.shape["sgroup"], mesh.shape["tile"]
    in_specs = (
        P(None, "sgroup", "tile", None, None, None),
        P(None, "sgroup", None, None, None),
        P("sgroup", "tile"),
        P(),
    )
    run = functools.partial(body, groups, owners)
    return jax.shard_map(run, mesh=mesh, in_specs=in_specs, out_specs=P("tile", None, "sgroup", None), check_vma=False)
```

```python
import functools

import jax
import jax.numpy as jnp
from jax import lax
from jax.experimental import pallas as pl
from jax.experimental.pallas import tpu as pltpu
from jax.sharding import PartitionSpec as P


F32, BF16 = jnp.float32, jnp.bfloat16


def iota(shape, axis):
    return lax.broadcasted_iota(jnp.int32, shape, axis)


def dot(left, right):
    return jnp.dot(left, right, preferred_element_type=F32)


def beam_kernel(owners, index_hbm, w_hbm, v_hbm, keep_ref, send_ref, index_ref, w_ref, v_ref, left_ref, acc_ref, small_sem, v_sem):
    _, stations, antennas, polars, channels, spectra = v_ref.shape
    numbers = w_ref.shape[-1]
    per_owner = channels // owners
    rows = 2 * channels
    me = lax.axis_index("tile").astype(jnp.int32)
    copies = [pltpu.make_async_copy(index_hbm, index_ref, small_sem.at[0]), pltpu.make_async_copy(w_hbm, w_ref, small_sem.at[1])]
    spans = [(s, min(s + 2, stations)) for s in range(0, stations - 2, 2)] + [(s, s + 1) for s in range(max(stations - 2, 0), stations)]
    arrivals = {a: pltpu.make_async_copy(v_hbm.at[:, a:b], v_ref.at[:, a:b], v_sem.at[a]) for a, b in spans}
    for copy in copies:
        copy.start(priority=0)
    for copy in arrivals.values():
        copy.start(priority=1)

    spread = jnp.where(iota((antennas, antennas * channels), 1) // channels == iota((antennas, antennas * channels), 0), 1.0, 0.0).astype(BF16)
    lane_tile = min(128, antennas * channels)
    mask = iota((rows, lane_tile), 1) % channels == iota((rows, lane_tile), 0) % channels
    number = iota((numbers, antennas), 0)
    for copy in copies:
        copy.wait()
    compact = []
    for s in range(stations):
        chosen = jnp.where(number == index_ref[s : s + 1, :], 1.0, 0.0).astype(BF16)
        lines = jnp.concatenate([w_ref[k, s, p] for p in range(polars) for k in range(2)], axis=0)
        compact.append(dot(lines, chosen).astype(BF16))
    for s in range(stations):
        wide = dot(compact[s], spread)
        for p in range(polars):
            for i in range(0, antennas * channels, lane_tile):
                part = wide[p * rows : (p + 1) * rows, i : i + lane_tile]
                left_ref[s, p, :, i : i + lane_tile] = jnp.where(mask, part, 0.0).astype(BF16)

    def order_rows(stop, size):
        for slot in range(owners):
            target = send_ref if slot % 2 else keep_ref
            first = (stop - size) * polars * rows + (me ^ slot) * per_owner
            for part in range(2):
                for c in range(per_owner):
                    line = acc_ref[pl.ds(first + part * channels + c, size * polars, stride=rows), :]
                    target[slot // 2, part * per_owner + c, (stop - size) * polars : stop * polars] = line.astype(target.dtype)

    batch = 4 if stations % 4 == 0 else stations
    for s in range(stations):
        if s in arrivals:
            arrivals[s].wait()
        for p in range(polars):
            left = left_ref[s, p]
            real = dot(left, v_ref[0, s, :, p].reshape(antennas * channels, spectra))
            imag = dot(left, v_ref[1, s, :, p].reshape(antennas * channels, spectra))
            at = (s * polars + p) * rows
            acc_ref[at : at + channels, :] = real[:channels] - imag[channels:]
            acc_ref[at + channels : at + rows, :] = real[channels:] + imag[:channels]
        if (s + 1) % batch == 0:
            order_rows(s + 1, batch)


def beam(owners, index, weights, voltages):
    _, stations, antennas, polars, channels, spectra = voltages.shape
    rows = 2 * channels
    half = (owners // 2, rows // owners, stations * polars, spectra)
    hbm, vmem = pl.BlockSpec(memory_space=pltpu.HBM), pl.BlockSpec(memory_space=pltpu.VMEM)
    return pl.pallas_call(
        functools.partial(beam_kernel, owners),
        out_shape=(jax.ShapeDtypeStruct(half, F32), jax.ShapeDtypeStruct(half, BF16)),
        in_specs=[hbm, hbm, hbm],
        out_specs=[vmem, vmem],
        scratch_shapes=[
            pltpu.VMEM(index.shape, jnp.int32),
            pltpu.VMEM(weights.shape, BF16),
            pltpu.VMEM(voltages.shape, BF16),
            pltpu.VMEM((stations, polars, rows, antennas * channels), BF16),
            pltpu.VMEM((stations * polars * rows, spectra), F32),
            pltpu.SemaphoreType.DMA((2,)),
            pltpu.SemaphoreType.DMA((stations,)),
        ],
        compiler_params=pltpu.CompilerParams(vmem_limit_bytes=48 << 20),
        name="beam",
    )(*(pltpu.with_memory_space_constraint(a, pltpu.HBM) for a in (index, weights, voltages)))


def place_kernel(local, polars, order_ref, place_ref):
    total, stations = place_ref.shape[0], order_ref.shape[1]
    owns = jnp.where(order_ref[...] == iota((total, stations), 0) // polars, 1.0, 0.0).astype(BF16)
    column = iota((stations, total), 1)
    block, far = column // local, total // local // 2
    block = jnp.where(block == far, far - 1, jnp.where(block == far - 1, far, block))
    slot = (block ^ lax.axis_index("sgroup").astype(jnp.int32)) * (local // polars) + (column % local) // polars
    slots = jnp.where(iota((stations, total), 0) == slot, 1.0, 0.0).astype(BF16)
    same = iota((total, total), 0) % polars == iota((total, total), 1) % polars
    place_ref[...] = jnp.where(same, dot(owns, slots), 0.0).astype(BF16)


def placement(order, polars, local):
    vmem = pl.BlockSpec(memory_space=pltpu.VMEM)
    total = order.shape[0] * polars
    return pl.pallas_call(
        functools.partial(place_kernel, local, polars),
        out_shape=jax.ShapeDtypeStruct((total, total), BF16),
        in_specs=[vmem],
        out_specs=vmem,
        compiler_params=pltpu.CompilerParams(vmem_limit_bytes=48 << 20),
        name="place",
    )(order[None, :])


def both_parts(blocks, c, channels):
    real = jnp.concatenate([b[c] for b in blocks], axis=0)
    imag = jnp.concatenate([b[channels + c] for b in blocks], axis=0)
    return jnp.concatenate([real, imag], axis=1)


def early_kernel(place_ref, *refs):
    blocks, row_ref = refs[:-1], refs[-1]
    place = place_ref[:, : place_ref.shape[1] // 2]
    channels = row_ref.shape[0]
    for c in range(channels):
        row_ref[c] = dot(place, both_parts(blocks, c, channels)).astype(BF16)


def early(place, blocks):
    inner, _, spectra = blocks[0].shape
    vmem = pl.BlockSpec(memory_space=pltpu.VMEM)
    return pl.pallas_call(
        early_kernel,
        out_shape=jax.ShapeDtypeStruct((inner // 2, place.shape[0], 2 * spectra), BF16),
        in_specs=[vmem] * (1 + len(blocks)),
        out_specs=vmem,
        compiler_params=pltpu.CompilerParams(vmem_limit_bytes=48 << 20),
        name="early",
    )(place, *blocks)


def correlate_kernel(place_ref, early_ref, *refs):
    blocks, (out_hbm, row_ref, out_ref, sem) = refs[:-4], refs[-4:]
    inner, local, spectra = blocks[0].shape
    channels = inner // 2
    me, place = lax.axis_index("sgroup").astype(jnp.int32), place_ref[:, place_ref.shape[1] // 2 :]
    scale = 1.0 / spectra
    for c in range(channels):
        row_ref[c] = dot(place, both_parts(blocks, c, channels)).astype(BF16) + early_ref[c]
    rows, copies = pl.ds(pl.multiple_of(me * local, local), local), []
    for c in range(channels):
        mine = row_ref[c, rows, :]
        left = jnp.concatenate(
            [mine, jnp.concatenate([mine[:, spectra:], -mine[:, :spectra]], axis=1)], axis=0
        )
        vis = lax.dot_general(left, row_ref[c], (((1,), (1,)), ((), ())), preferred_element_type=F32) * scale
        out_ref[c, 0] = vis[:local]
        out_ref[c, 1] = vis[local:]
        copies.append(pltpu.make_async_copy(out_ref.at[c], out_hbm.at[c], sem.at[c]))
        copies[-1].start()
    for copy in copies:
        copy.wait()


def correlate(place, ordered, blocks):
    inner, local, spectra = blocks[0].shape
    total = place.shape[0]
    shape = (inner // 2, 2, local, total)
    vmem = pl.BlockSpec(memory_space=pltpu.VMEM)
    return pl.pallas_call(
        correlate_kernel,
        out_shape=jax.ShapeDtypeStruct(shape, F32),
        in_specs=[vmem] * (2 + len(blocks)),
        out_specs=pl.BlockSpec(memory_space=pltpu.HBM),
        scratch_shapes=[
            pltpu.VMEM((inner // 2, total, 2 * spectra), BF16),
            pltpu.VMEM(shape, F32),
            pltpu.SemaphoreType.DMA((inner // 2,)),
        ],
        compiler_params=pltpu.CompilerParams(vmem_limit_bytes=48 << 20),
        name="correlate",
    )(place, ordered, *blocks)


def body(groups, owners, voltages, weights, antenna_slot_index, station_order):
    far = groups // 2

    def exchange(value, axis, size, bit):
        return lax.ppermute(value, axis, [(i, i ^ bit) for i in range(size)])

    def share(value, bit):
        return exchange(value, "sgroup", groups, bit)

    keep, send = beam(owners, antenna_slot_index, jnp.transpose(weights, (0, 1, 3, 4, 2)), voltages)
    total = keep + exchange(send, "tile", owners, 1).astype(F32)
    bit = 2
    while bit < owners:
        sent = total[1::2].astype(F32 if 2 * bit < owners else BF16)
        sent = exchange(sent, "tile", owners, bit)
        total = total[0::2] + sent.astype(F32)
        bit *= 2
    own = total[0].astype(BF16)
    blocks = {0: own, far: share(own, far)}
    for i in range(far - 2, 0, -1):
        blocks[i] = share(own, i)
    both = share(jnp.stack([own, blocks[far]]), far - 1)
    blocks[far - 1], blocks[far + far - 1] = both[0], both[1]
    for i in range(1, far - 1):
        blocks[far + i] = share(blocks[far], i)
    place = placement(station_order, voltages.shape[3], own.shape[1])
    first = [*range(far - 1), far]
    ordered = early(place, [blocks[i] for i in first])
    return correlate(place, ordered, [blocks[i] for i in range(groups) if i not in first])


def solution(mesh):
    groups, owners = mesh.shape["sgroup"], mesh.shape["tile"]
    in_specs = (
        P(None, "sgroup", "tile", None, None, None),
        P(None, "sgroup", None, None, None),
        P("sgroup", "tile"),
        P(),
    )
    run = functools.partial(body, groups, owners)
    return jax.shard_map(run, mesh=mesh, in_specs=in_specs, out_specs=P("tile", None, "sgroup", None), check_vma=False)
```
